512 devices in a mesh: src: 32 (over y_lo, z), dst: 16 (over x, y_hi, core).
Axes of the slice: x: 4, y: 4 (y_hi: 2, y_lo: 2; y = y_hi * 2 + y_lo), z: 16, core: 2. Of those that a mesh axis runs over, the one named last changes fastest.
Arguments:
- features: bfloat16 [65536, 128], P(('src', 'dst')), may hold values from -6 to 6
- weight: bfloat16 [128, 256], replicated, may hold values from -0.5 to 0.5
- bias: float32 [256], replicated, may hold values from -3 to 3
- tile_index: int32 [32, 16, 128], P('src', 'dst'), may hold values from 0 to 511, as said below
- edge_count: int32 [32, 16, 128], P('src', 'dst'), may hold values from 0 to 64, as said below
- edge_pos: int32 [32, 16, 128, 64], P('src', 'dst'), may hold values from 0 to 16383
- edge_weight: bfloat16 [32, 16, 128, 64], P('src', 'dst'), may hold values from 0.099609375 to 0.3984375
- grad_out: bfloat16 [65536, 256], P(('src', 'dst')), may hold values from -15 to 15
Outputs:
- hidden: bfloat16 [65536, 256], P(('src', 'dst'))
- input_grad: bfloat16 [65536, 128], P(('src', 'dst'))
- weight_grad: float32 [128, 256], replicated
- bias_grad: float32 [256], replicated
The draws below stay inside these ranges and needn't reach their ends.
Inputs may be any that keep to these rules, and one draw needn't show every extreme that they name: `tile_index`: the 128 entries of one device are distinct; id c names tile row c // 16 and tile column c % 16 of the device's block of 4096 target rows and 2048 source columns. `edge_count`: on each device the live slots (count 1 or more) come first and all later slots have count 0; slot 0 is always live; some device has all 128 slots live; every device has a slot with 64 edges. `edge_pos`: row * 128 + column inside the tile; positions may repeat within a tile.
All inputs are finite; a program needn't handle non-finite values.
Results may differ from the reference program's by a relative error of at most 0.0065.
Values may be sent and summed in bfloat16 or wider, within the bound.
No kernel may reach another device: no remote copies, remote signals or barrier semaphores. Data moves between devices by JAX's collectives and lax.ppermute only.
A program may use at most 64 MiB of HBM per device.

```python
import math
import jax
import jax.numpy as jnp
from jax import lax

F_IN = 128
F_HID = 256
NODE_DEV = 128
TILE = 128
EDGE_TILE = 64
SRC_ROWS = 2048
SRC_TILES = 16
DST_TILES = 32
TILES_DEV = 128
NODES = 65536
N_SRC = 32
N_DST = 16


def live_tiles(key):
    first_draw = jax.random.randint(jax.random.fold_in(key, 11), (N_SRC, N_DST), 0, TILES_DEV + 1)
    second = jax.random.randint(jax.random.fold_in(key, 12), (N_SRC, N_DST), 0, TILES_DEV + 1)
    live_count = jnp.maximum(max(TILES_DEV // 8, 1), first_draw * second // TILES_DEV)
    busiest = jax.random.randint(jax.random.fold_in(key, 13), (), 0, N_SRC * N_DST)
    flat_live = live_count.reshape(-1)
    flat_live = jnp.where(jnp.arange(N_SRC * N_DST, dtype=jnp.int32) == busiest, TILES_DEV, flat_live)
    return flat_live.reshape(N_SRC, N_DST)


def draw_tile_index(key, part):
    slot_total = SRC_TILES * DST_TILES
    scores = jax.random.randint(key, (N_SRC, N_DST, slot_total), 0, 1 << 16) * slot_total + jnp.arange(slot_total, dtype=jnp.int32)
    ordering = jnp.argsort(scores, axis=-1)
    return ordering[:, :, :TILES_DEV].astype(jnp.int32)


def draw_edge_count(key, part):
    live_count = live_tiles(key)
    counts = jax.random.randint(jax.random.fold_in(key, 21), (N_SRC, N_DST, TILES_DEV), 1, EDGE_TILE + 1)
    fullest = jax.random.randint(jax.random.fold_in(key, 22), (N_SRC, N_DST), 0, 1 << 20) % live_count
    slot_ids = jnp.arange(TILES_DEV, dtype=jnp.int32)
    counts = jnp.where(slot_ids[None, None, :] == fullest[:, :, None], EDGE_TILE, counts)
    return jnp.where(slot_ids[None, None, :] < live_count[:, :, None], counts, 0).astype(jnp.int32)


def draw_grad_out(key, part):
    row_ramp = jnp.exp(jnp.log(3.0) * jnp.arange(NODES, dtype=jnp.float32) / (NODES - 1))
    values = jnp.clip(jax.random.normal(key, (NODES, F_HID), jnp.float32), -5.0, 5.0)
    return (values * row_ramp[:, None]).astype(jnp.bfloat16)


def place_ends(values, key, least, high):
    longest = values.shape.index(max(values.shape))
    spots = []
    for shift in (0, 1):
        where = [jax.random.randint(jax.random.fold_in(key, axis), (), 0, length) for axis, length in enumerate(values.shape)]
        where[longest] = (where[longest] + shift) % values.shape[longest]
        spots.append(tuple(where))
    return values.at[spots[0]].set(least).at[spots[1]].set(high)


def shard_levels(rng, dims, shards, smallest, largest):
    def one(dim, blocks):
        draws = jax.random.uniform(jax.random.fold_in(jax.random.fold_in(rng, 6), dim), (blocks,), jnp.float32, smallest / len(shards), largest / len(shards))
        return jnp.repeat(jnp.exp(draws), dims[dim] // blocks).reshape((-1,) + (1,) * (len(dims) - dim - 1))

    loudness = one(*shards[0])
    for cut in shards[1:]:
        loudness = loudness * one(*cut)
    return loudness


def noise(stream_key, dims, spread, reach, split=(), kind=jnp.bfloat16):
    values = spread * jax.random.normal(stream_key, dims, jnp.float32)
    if split:
        values = values * shard_levels(stream_key, dims, split, -0.22, 0.18)
    return jnp.clip(values, -reach, reach).astype(kind)


def setup_inputs(seed: int = 0) -> dict:
    keys = jax.random.split(jax.random.key(seed), 9)
    features = noise(keys[0], (NODES, F_IN), 1.0, 6.0, ((0, 512),))
    weight = noise(keys[1], (F_IN, F_HID), F_IN ** -0.5, 0.5)
    bias = noise(keys[2], (F_HID,), 0.5, 3.0, (), jnp.float32)
    tile_index = draw_tile_index(jax.random.fold_in(keys[8], 71), 0)
    edge_count = draw_edge_count(jax.random.fold_in(keys[8], 71), 0)
    edge_pos = place_ends(jax.random.randint(keys[5], (N_SRC, N_DST, TILES_DEV, EDGE_TILE), 0, TILE * TILE), jax.random.fold_in(keys[5], 1), 0, (TILE * TILE) - 1).astype(jnp.int32)
    edge_weight = jnp.clip(jnp.exp(math.log(0.3984375) - 1.3862944 * jax.random.uniform(keys[6], (N_SRC, N_DST, TILES_DEV, EDGE_TILE), jnp.float32) ** shard_levels(keys[6], (N_SRC, N_DST, TILES_DEV, EDGE_TILE), ((0, 32), (1, 16)), -0.2, 0.2)), 0.099609375, 0.3984375).astype(jnp.bfloat16)
    grad_out = draw_grad_out(jax.random.fold_in(keys[8], 71), 0)
    return dict(features=features, weight=weight, bias=bias, tile_index=tile_index, edge_count=edge_count, edge_pos=edge_pos, edge_weight=edge_weight, grad_out=grad_out)


def edge_values(positions, weights, counts):
    slot_ids = jnp.arange(positions.shape[1], dtype=jnp.int32)
    live_mask = slot_ids[None, :] < counts[:, None]
    paired = (positions[:, :, None] == positions[:, None, :]) & live_mask[:, :, None] & live_mask[:, None, :]
    summed = lax.optimization_barrier(jnp.sum(jnp.where(paired, weights.astype(jnp.float32)[:, None, :], jnp.zeros((), jnp.float32)), axis=2))
    repeated = jnp.any(paired & (slot_ids[None, :, None] > slot_ids[None, None, :]), axis=2)
    rounded = lax.optimization_barrier(summed.astype(jnp.bfloat16)).astype(jnp.float32)
    return jnp.where(live_mask & jnp.logical_not(repeated), rounded, jnp.zeros((), jnp.float32))

def device_edges(device_index, tile_index, edge_count, edge_pos, edge_weight):
    src_part = device_index // N_DST
    dst_part = device_index % N_DST
    tile_ids = tile_index.reshape(-1, TILES_DEV)[device_index]
    counts = edge_count.reshape(-1, TILES_DEV)[device_index]
    positions = edge_pos.reshape(-1, TILES_DEV, EDGE_TILE)[device_index]
    weights = edge_weight.reshape(-1, TILES_DEV, EDGE_TILE)[device_index]
    values = edge_values(positions, weights, counts)
    local_source = (tile_ids % SRC_TILES)[:, None] * TILE + positions % TILE
    local_target = (tile_ids // SRC_TILES)[:, None] * TILE + positions // TILE
    sources = src_part * SRC_ROWS + local_source
    targets = local_target // NODE_DEV * SRC_ROWS + dst_part * NODE_DEV + local_target % NODE_DEV
    return (sources.reshape(-1).astype(jnp.int32), targets.reshape(-1).astype(jnp.int32), values.reshape(-1))

def reference(features, weight, bias, tile_index, edge_count, edge_pos, edge_weight, grad_out):
    device_ids = jnp.arange(N_SRC * N_DST, dtype=jnp.int32)
    source_values = features.astype(jnp.float32)

    def forward_step(running, device_index):
        sources, targets, values = device_edges(device_index, tile_index, edge_count, edge_pos, edge_weight)
        return (running.at[targets].add(values[:, None] * source_values[sources]), None)
    summed, _ = lax.scan(forward_step, jnp.zeros((NODES, F_IN), jnp.float32), device_ids)
    aggregated = summed.astype(jnp.bfloat16)
    preact = jnp.dot(aggregated, weight, preferred_element_type=jnp.float32) + bias
    hidden = jax.nn.silu(preact).astype(jnp.bfloat16)
    sigmoid_pre = jax.nn.sigmoid(preact)
    grad_pre = (grad_out.astype(jnp.float32) * sigmoid_pre * (1.0 + preact * (1.0 - sigmoid_pre))).astype(jnp.bfloat16)
    node_scale = 1.0 / math.sqrt(NODES)
    weight_grad = jnp.dot(aggregated.T, grad_pre, preferred_element_type=jnp.float32) * node_scale
    bias_grad = lax.optimization_barrier(jnp.sum(grad_pre.astype(jnp.float32), axis=0)) * node_scale
    back_rows = jnp.dot(grad_pre, weight.T, preferred_element_type=jnp.float32).astype(jnp.bfloat16)
    back_values = back_rows.astype(jnp.float32)

    def backward_step(running, device_index):
        sources, targets, values = device_edges(device_index, tile_index, edge_count, edge_pos, edge_weight)
        return (running.at[sources].add(values[:, None] * back_values[targets]), None)
    back_summed, _ = lax.scan(backward_step, jnp.zeros((NODES, F_IN), jnp.float32), device_ids)
    input_grad = back_summed.astype(jnp.bfloat16)
    return (hidden, input_grad, weight_grad, bias_grad)
```

```python
import math

import jax
import jax.numpy as jnp
from jax import lax
from jax.experimental import pallas as pl
from jax.experimental.pallas import tpu as pltpu
from jax.sharding import PartitionSpec as P

TILE = 128
BF16 = jnp.bfloat16
F32 = jnp.float32
NT = (((1,), (1,)), ((), ()))
TN = (((0,), (0,)), ((), ()))


def dot(a, b, dims=(((1,), (0,)), ((), ()))):
    return lax.dot_general(a, b, dims, preferred_element_type=F32)


def build_kernel(count_ref, pos_ref, weight_ref, tile_ref, back_ref, pos_pairs, weight_pairs):
    pairs = pos_pairs.shape[0]
    edges = pos_ref.shape[1]
    pos_pairs[...] = jnp.concatenate([pos_ref[:pairs, :], pos_ref[pairs:, :]], axis=1)
    weight_pairs[...] = jnp.concatenate(
        [weight_ref[:pairs, :].astype(F32), weight_ref[pairs:, :].astype(F32)], axis=1
    )
    lane = lax.broadcasted_iota(jnp.int32, (1, 2 * edges), 1)
    second = lane >= edges
    half = jnp.where(second, TILE, 0)
    one_rows = lax.broadcasted_iota(jnp.int32, (TILE, 2 * edges), 0)
    two_rows = lax.broadcasted_iota(jnp.int32, (2 * TILE, 2 * edges), 0)

    def one_pair(i, carry):
        limit = jnp.where(second, count_ref[i + pairs] + edges, count_ref[i])
        position = pos_pairs[pl.ds(i, 1), :]
        values = jnp.where(lane < limit, weight_pairs[pl.ds(i, 1), :], 0.0)
        row = position >> 7
        col = position & (TILE - 1)
        row_hot = jnp.where(one_rows == row, values, 0.0).astype(BF16)
        col_pair = jnp.where(two_rows == col + half, 1.0, 0.0).astype(BF16)
        tile_ref[i] = dot(row_hot, col_pair, NT).astype(BF16)
        col_hot = jnp.where(one_rows == col, 1.0, 0.0).astype(BF16)
        row_pair = jnp.where(two_rows == row + half, values, 0.0).astype(BF16)
        back_ref[i] = dot(col_hot, row_pair, NT).astype(BF16)
        return carry

    lax.fori_loop(0, pairs, one_pair, 0, unroll=2)


def forward_kernel(index_ref, tile_ref, source_ref, out_ref, sums):
    pairs = tile_ref.shape[0]
    source_tiles = source_ref.shape[0]
    shift = source_tiles.bit_length() - 1
    sums[...] = jnp.zeros_like(sums)

    def one_step(step, carry):
        found = []
        for j in range(4):
            i = step * 4 + j
            for part in range(2):
                index = index_ref[i + part * pairs]
                tile = tile_ref[i, :, part * TILE : (part + 1) * TILE]
                found.append((index >> shift, dot(tile, source_ref[index & (source_tiles - 1)])))
        for target, value in found:
            sums[target] = sums[target] + value
        return carry

    lax.fori_loop(0, pairs // 4, one_step, 0)
    out_ref[...] = sums[...].astype(BF16)


def backward_kernel(index_ref, tile_ref, recv_ref, out_ref, chunk_ref, bias_ref, sums):
    pairs = tile_ref.shape[0]
    source_tiles = out_ref.shape[0]
    shift = source_tiles.bit_length() - 1
    sums[...] = jnp.zeros_like(sums)

    def one_step(step, carry):
        found = []
        for j in range(4):
            i = step * 4 + j
            for part in range(2):
                index = index_ref[i + part * pairs]
                tile = tile_ref[i, :, part * TILE : (part + 1) * TILE]
                rows = recv_ref[index >> shift, :TILE, :]
                found.append((index & (source_tiles - 1), dot(tile, rows)))
        for source, value in found:
            sums[source] = sums[source] + value
        return carry

    lax.fori_loop(0, pairs // 4, one_step, 0)
    out_ref[...] = sums[...].astype(BF16)
    extra = jnp.sum(recv_ref[:, TILE:, :].astype(F32), axis=0)
    chunk_ref[...] = extra[0:8] + extra[8:16]
    bias_ref[...] = extra[16:24] + extra[24:32]


def dense_kernel(recv_ref, weight_ref, bias_ref, grad_ref, hidden_ref, send_ref):
    peers = recv_ref.shape[0]
    aggregated = jnp.sum(recv_ref[...].astype(F32), axis=0).astype(BF16)
    weight = weight_ref[...]
    preact = dot(aggregated, weight) + bias_ref[...]
    sigma = 1.0 / (1.0 + jnp.exp(-preact))
    hidden_ref[...] = (preact * sigma).astype(BF16)
    grad_pre = (grad_ref[...].astype(F32) * sigma * (1.0 + preact * (1.0 - sigma))).astype(BF16)
    back_rows = dot(grad_pre, weight, NT).astype(BF16)
    send_ref[:, 0:TILE, :] = jnp.broadcast_to(back_rows[None], (peers, TILE, TILE))
    weight_part = dot(aggregated, grad_pre, TN)
    chunks = jnp.concatenate(
        [weight_part[:, :TILE].reshape(peers // 2, 8, TILE), weight_part[:, TILE:].reshape(peers // 2, 8, TILE)], axis=0
    )
    chunk_high = chunks.astype(BF16)
    chunk_low = (chunks - chunk_high.astype(F32)).astype(BF16)
    bias_part = jnp.sum(grad_pre.astype(F32), axis=0, keepdims=True)
    sub = lax.broadcasted_iota(jnp.int32, (8, TILE), 0)
    bias_rows = jnp.where(sub == 0, bias_part[:, :TILE], jnp.where(sub == 1, bias_part[:, TILE:], 0.0))
    bias_high = bias_rows.astype(BF16).astype(F32)
    bias_low = bias_rows - bias_high
    bias_both = jnp.concatenate([bias_high, bias_low], axis=0).astype(BF16)
    send_ref[:, TILE : TILE + 16, :] = jnp.concatenate([chunk_high, chunk_low], axis=1)
    send_ref[:, TILE + 16 :, :] = jnp.broadcast_to(bias_both[None], (peers, 16, TILE))


def vmem(n):
    return [pl.BlockSpec(memory_space=pltpu.VMEM)] * n


def smem(n):
    return [pl.BlockSpec(memory_space=pltpu.SMEM)] * n


def body(features, weight, bias, tile_index, edge_count, edge_pos, edge_weight, grad_out):
    src = lax.axis_size("src")
    dst = lax.axis_size("dst")
    index = tile_index.reshape(-1)
    counts = edge_count.reshape(-1)
    slots = counts.shape[0]
    positions = edge_pos.reshape(slots, -1)
    weights = edge_weight.reshape(slots, -1)
    edges = positions.shape[1]
    pairs = slots // 2
    params = pltpu.CompilerParams(vmem_limit_bytes=56 << 20)

    sent = jnp.broadcast_to(features[None], (dst,) + features.shape)
    source_tiles = lax.all_to_all(sent, "dst", 0, 0, tiled=True)
    pair_shape = jax.ShapeDtypeStruct((pairs, TILE, 2 * TILE), BF16)
    tiles, back_tiles = pl.pallas_call(
        build_kernel,
        out_shape=(pair_shape, pair_shape),
        in_specs=smem(1) + vmem(2),
        out_specs=tuple(vmem(2)),
        scratch_shapes=[pltpu.VMEM((pairs, 2 * edges), jnp.int32), pltpu.VMEM((pairs, 2 * edges), F32)],
        compiler_params=params,
        name="build_tiles",
    )(counts, positions, weights)
    partial = pl.pallas_call(
        forward_kernel,
        out_shape=jax.ShapeDtypeStruct((src, TILE, TILE), BF16),
        in_specs=smem(1) + vmem(2),
        out_specs=vmem(1)[0],
        scratch_shapes=[pltpu.VMEM((src, TILE, TILE), F32)],
        compiler_params=params,
        name="forward_tiles",
    )(index, tiles, source_tiles)
    parts = lax.all_to_all(partial, "src", 0, 0, tiled=True)
    hidden, send = pl.pallas_call(
        dense_kernel,
        out_shape=(
            jax.ShapeDtypeStruct(grad_out.shape, BF16),
            jax.ShapeDtypeStruct((src, TILE + 32, TILE), BF16),
        ),
        in_specs=vmem(4),
        out_specs=tuple(vmem(2)),
        compiler_params=params,
        name="dense_layer",
    )(parts, weight, bias.reshape(1, -1), grad_out)
    received = lax.all_to_all(send, "src", 0, 0, tiled=True)
    back_partial, chunk, bias_rows = pl.pallas_call(
        backward_kernel,
        out_shape=(
            jax.ShapeDtypeStruct((dst, TILE, TILE), BF16),
            jax.ShapeDtypeStruct((8, TILE), F32),
            jax.ShapeDtypeStruct((8, TILE), F32),
        ),
        in_specs=smem(1) + vmem(2),
        out_specs=tuple(vmem(3)),
        scratch_shapes=[pltpu.VMEM((dst, TILE, TILE), F32)],
        compiler_params=params,
        name="backward_tiles",
    )(index, back_tiles, received)
    back_parts = lax.all_to_all(back_partial, "dst", 0, 0, tiled=True)
    input_grad = jnp.sum(back_parts.astype(F32), axis=0).astype(BF16)
    node_scale = 1.0 / math.sqrt(features.shape[0] * src * dst)
    both = jnp.concatenate([chunk, bias_rows], axis=0)
    both = lax.all_to_all(jnp.broadcast_to(both[None], (dst, 16, TILE)), "dst", 0, 0, tiled=True)
    both = jnp.sum(both, axis=0) * node_scale
    spread = lax.all_to_all(jnp.broadcast_to(both[None, :8], (src, 8, TILE)), "src", 0, 0, tiled=True)
    weight_grad = jnp.concatenate(
        [spread[: src // 2].reshape(TILE, TILE), spread[src // 2 :].reshape(TILE, TILE)], axis=1
    )
    bias_grad = both[8:10].reshape(-1)
    return (hidden, input_grad, weight_grad, bias_grad)


def solution(mesh):
    placed = (
        P(("src", "dst"), None),
        P(),
        P(),
        P("src", "dst", None),
        P("src", "dst", None),
        P("src", "dst", None, None),
        P("src", "dst", None, None),
        P(("src", "dst"), None),
    )
    return jax.shard_map(
        body,
        mesh=mesh,
        in_specs=placed,
        out_specs=(P(("src", "dst"), None), P(("src", "dst"), None), P(), P()),
        check_vma=False,
    )
```

```python
import math

import jax
import jax.numpy as jnp
from jax import lax
from jax.experimental import pallas as pl
from jax.experimental.pallas import tpu as pltpu
from jax.sharding import Mesh, PartitionSpec as P

TILE = 128
BF16 = jnp.bfloat16
F32 = jnp.float32
NN = (((1,), (0,)), ((), ()))
NT = (((1,), (1,)), ((), ()))
TN = (((0,), (0,)), ((), ()))
SRC = ("ylo", "zq", "z0")
NEAR = ("ylo", "z0")
FAR = "zq"
UNROLL = 8


def dot(a, b, dims=NN):
    return lax.dot_general(a, b, dims, preferred_element_type=F32)


def build_kernel(count_ref, pos_ref, weight_ref, tile_ref, pos_pairs, weight_pairs, *, backward):
    edges, slots = pos_ref.shape
    pairs = slots // 2
    positions = pos_ref[...].T
    weights = weight_ref[...].astype(F32).T
    pos_pairs[...] = jnp.concatenate([positions[:pairs], positions[pairs:]], axis=1)
    weight_pairs[...] = jnp.concatenate([weights[:pairs], weights[pairs:]], axis=1)
    lane = lax.broadcasted_iota(jnp.int32, (1, 2 * edges), 1)
    second = lane >= edges
    half = jnp.where(second, TILE, 0)
    one_rows = lax.broadcasted_iota(jnp.int32, (TILE, 2 * edges), 0)
    two_rows = lax.broadcasted_iota(jnp.int32, (2 * TILE, 2 * edges), 0)

    def one_pair(i, carry):
        limit = jnp.where(second, count_ref[i + pairs] + edges, count_ref[i])
        position = pos_pairs[pl.ds(i, 1), :]
        values = jnp.where(lane < limit, weight_pairs[pl.ds(i, 1), :], 0.0)
        row = position >> 7
        col = position & (TILE - 1)
        if backward:
            left = jnp.where(one_rows == col, 1.0, 0.0).astype(BF16)
            right = jnp.where(two_rows == row + half, values, 0.0).astype(BF16)
        else:
            left = jnp.where(one_rows == row, values, 0.0).astype(BF16)
            right = jnp.where(two_rows == col + half, 1.0, 0.0).astype(BF16)
        both = dot(left, right, NT).astype(BF16)
        tile_ref[i] = both[:, :TILE]
        tile_ref[i + pairs] = both[:, TILE:]
        return carry

    lax.fori_loop(0, pairs, one_pair, 0, unroll=4)


def spread_tiles(from_ref, into_ref, tile_ref, rows_ref, sums):
    sums[...] = jnp.zeros_like(sums)

    def one_step(step, carry):
        found = []
        for j in range(UNROLL):
            i = step * UNROLL + j
            found.append((into_ref[i], dot(tile_ref[i], rows_ref[from_ref[i]])))
        for target, value in found:
            sums[target] = sums[target] + value
        return carry

    lax.fori_loop(0, tile_ref.shape[0] // UNROLL, one_step, 0)


def forward_kernel(from_ref, into_ref, tile_ref, rows_ref, own_ref, *rest):
    sums = rest[-1]
    far = own_ref.shape[0]
    spread_tiles(from_ref, into_ref, tile_ref, rows_ref, sums)
    own_ref[...] = sums[:far]
    for k, out_ref in enumerate(rest[:-1]):
        out_ref[...] = sums[(k + 1) * far : (k + 2) * far].astype(BF16)


def add_kernel(own_ref, *rest):
    total = own_ref[...]
    for recv_ref in rest[:-1]:
        total = total + recv_ref[...].astype(F32)
    rest[-1][...] = total.astype(BF16)


def high_low(value):
    high = value.astype(BF16).astype(F32)
    return high, value - high


def bias_tile(bias_rows):
    return jnp.concatenate(high_low(bias_rows), axis=0).astype(BF16)


def dense_kernel(recv_ref, weight_ref, bias_ref, grad_ref, hidden_ref, send_ref):
    peers = recv_ref.shape[0]
    aggregated = jnp.sum(recv_ref[...].astype(F32), axis=0).astype(BF16)
    weight = weight_ref[...]
    preact = dot(aggregated, weight) + bias_ref[...]
    sigma = 1.0 / (1.0 + jnp.exp(-preact))
    hidden_ref[...] = (preact * sigma).astype(BF16)
    grad_pre = (grad_ref[...].astype(F32) * sigma * (1.0 + preact * (1.0 - sigma))).astype(BF16)
    back_rows = dot(grad_pre, weight, NT).astype(BF16)
    send_ref[:, :TILE, :] = jnp.broadcast_to(back_rows[None], (peers, TILE, TILE))
    part = dot(aggregated, grad_pre, TN).astype(BF16)
    rows = TILE // peers
    send_ref[:, TILE : TILE + rows, :] = part[:, :TILE].reshape(peers, rows, TILE)
    send_ref[:, TILE + rows : TILE + 2 * rows, :] = part[:, TILE:].reshape(peers, rows, TILE)
    bias_part = jnp.sum(grad_pre.astype(F32), axis=0, keepdims=True)
    sub = lax.broadcasted_iota(jnp.int32, (8, TILE), 0)
    bias_rows = jnp.where(sub == 0, bias_part[:, :TILE], jnp.where(sub == 1, bias_part[:, TILE:], 0.0))
    send_ref[:, TILE + 2 * rows :, :] = jnp.broadcast_to(bias_tile(bias_rows)[None], (peers, 16, TILE))


def middle_kernel(recv_ref, out_ref):
    peers = recv_ref.shape[0]
    top = peers * TILE
    out_ref[:top] = recv_ref[:, :TILE, :].reshape(top, TILE)
    total = jnp.sum(recv_ref[:, TILE:, :].astype(F32), axis=0)
    rows = total.shape[0] - 16
    high, low = high_low(total[:rows])
    out_ref[top : top + rows] = high.astype(BF16)
    out_ref[top + rows : top + 2 * rows] = low.astype(BF16)
    out_ref[top + 2 * rows :] = bias_tile(total[rows : rows + 8] + total[rows + 8 :])


def backward_kernel(from_ref, into_ref, tile_ref, *rest):
    near_refs, (out_ref, rows, sums) = rest[:-3], rest[-3:]
    far = rows.shape[0] // len(near_refs)
    top = far * TILE
    for k, near_ref in enumerate(near_refs):
        rows[k * far : (k + 1) * far] = near_ref[:top].reshape(far, TILE, TILE)
    spread_tiles(from_ref, into_ref, tile_ref, rows, sums)
    pieces = out_ref.shape[0]
    out_ref[:, :TILE, :] = sums[...].astype(BF16)
    total = near_refs[0][top:].astype(F32)
    for near_ref in near_refs[1:]:
        total = total + near_ref[top:].astype(F32)
    count = (total.shape[0] - 16) // 2
    chunk = (total[:count] + total[count : 2 * count]).astype(BF16)
    out_ref[:, TILE : TILE + count, :] = jnp.broadcast_to(chunk[None], (pieces, count, TILE))
    bias_rows = bias_tile(total[2 * count : 2 * count + 8] + total[2 * count + 8 :])
    out_ref[:, TILE + count :, :] = jnp.broadcast_to(bias_rows[None], (pieces, 16, TILE))


def input_kernel(recv_ref, input_ref, chunk_ref, bias_grad_ref, *, scale):
    input_ref[...] = jnp.sum(recv_ref[:, :TILE, :].astype(F32), axis=0).astype(BF16)
    total = jnp.sum(recv_ref[:, TILE:, :].astype(F32), axis=0) * scale
    count = total.shape[0] - 16
    chunk_ref[...] = jnp.broadcast_to(total[None, :count], chunk_ref.shape)
    bias_rows = total[count : count + 8] + total[count + 8 :]
    bias_grad_ref[:, :TILE] = bias_rows[0:1]
    bias_grad_ref[:, TILE:] = bias_rows[1:2]


def weight_kernel(recv_ref, weight_grad_ref):
    half = recv_ref.shape[1] // 2
    weight_grad_ref[:, :TILE] = recv_ref[:, :half, :].reshape(TILE, TILE)
    weight_grad_ref[:, TILE:] = recv_ref[:, half:, :].reshape(TILE, TILE)


def vmem(n):
    return [pl.BlockSpec(memory_space=pltpu.VMEM)] * n


def smem(n):
    return [pl.BlockSpec(memory_space=pltpu.SMEM)] * n


def call(kernel, name, outs, scalars, arrays, scratch=(), **more):
    single = not isinstance(outs, tuple)
    return pl.pallas_call(
        kernel,
        out_shape=outs,
        in_specs=smem(len(scalars)) + vmem(len(arrays)),
        out_specs=vmem(1)[0] if single else tuple(vmem(len(outs))),
        scratch_shapes=list(scratch),
        compiler_params=pltpu.CompilerParams(vmem_limit_bytes=56 << 20),
        name=name,
        **more,
    )(*scalars, *arrays)


def shape(dims, dtype):
    return jax.ShapeDtypeStruct(dims, dtype)


def swap(array, step, near):
    return lax.ppermute(array, NEAR, [(i, i ^ step) for i in range(near)])


def body(features, weight, bias, tile_index, edge_count, edge_pos, edge_weight, grad_out):
    near = lax.axis_size(NEAR)
    far = lax.axis_size(FAR)
    src = near * far
    dst = lax.axis_size("dst")
    index = tile_index.reshape(-1)
    counts = edge_count.reshape(-1)
    slots = counts.shape[0]
    positions = edge_pos.reshape(slots, -1).T
    weights = edge_weight.reshape(slots, -1).T
    edges = positions.shape[0]
    target = index // dst
    source = index % dst
    target_near = (target // (2 * far)) * 2 + target % 2
    place = (target_near ^ lax.axis_index(NEAR)) * far + (target // 2) % far
    tile_shape = shape((slots, TILE, TILE), BF16)
    block = shape((far, TILE, TILE), BF16)
    pair_scratch = (pltpu.VMEM((slots // 2, 2 * edges), jnp.int32), pltpu.VMEM((slots // 2, 2 * edges), F32))

    def build(positions, backward):
        return call(
            lambda *refs: build_kernel(*refs, backward=backward),
            "build_back" if backward else "build_tiles",
            tile_shape, (counts,), (positions, weights), pair_scratch,
        )

    sent = jnp.broadcast_to(features[None], (dst,) + features.shape)
    source_rows = lax.all_to_all(sent, "dst", 0, 0, tiled=True)
    tiles = build(positions, False)
    own, *others = call(
        forward_kernel,
        "forward_tiles",
        (shape(block.shape, F32),) + (block,) * (near - 1),
        (source, place),
        (tiles, source_rows),
        (pltpu.VMEM((src, TILE, TILE), F32),),
    )
    others = [swap(other, k + 1, near) for k, other in enumerate(others)]
    late_positions, own = lax.optimization_barrier((positions, own))
    back_tiles = build(late_positions, True)
    near_sums = call(add_kernel, "add_near", block, (), (own, *others))
    near_sums, back_tiles = lax.optimization_barrier((near_sums, back_tiles))
    parts = lax.all_to_all(near_sums, FAR, 0, 0, tiled=True)
    extra = 2 * TILE // far + 16
    hidden, send = call(
        dense_kernel,
        "dense_layer",
        (shape(grad_out.shape, BF16), shape((far, TILE + extra, TILE), BF16)),
        (),
        (parts, weight, bias.reshape(1, -1), grad_out),
    )
    far_rows = lax.all_to_all(send, FAR, 0, 0, tiled=True)
    near_rows = call(
        middle_kernel, "middle_sums", shape((far * TILE + 2 * extra - 16, TILE), BF16), (), (far_rows,)
    )
    near_all = [near_rows] + [swap(near_rows, k, near) for k in range(1, near)]
    back_send = call(
        backward_kernel,
        "backward_tiles",
        shape((dst, TILE + extra, TILE), BF16),
        (place, source),
        (back_tiles, *near_all),
        (pltpu.VMEM((src, TILE, TILE), BF16), pltpu.VMEM((dst, TILE, TILE), F32)),
    )
    received = lax.all_to_all(back_send, "dst", 0, 0, tiled=True)
    node_scale = 1.0 / math.sqrt(features.shape[0] * src * dst)
    input_grad, chunks, bias_grad = call(
        lambda *refs: input_kernel(*refs, scale=node_scale),
        "input_sums",
        (shape(features.shape, BF16), shape((far, extra - 16, TILE), F32), shape((1, 2 * TILE), F32)),
        (),
        (received,),
    )
    chunks = lax.all_to_all(chunks, FAR, 0, 0, tiled=True)
    weight_grad = call(weight_kernel, "weight_rows", shape((TILE, 2 * TILE), F32), (), (chunks,))
    return (hidden, input_grad, weight_grad, bias_grad.reshape(-1))


def solution(mesh):
    src, dst = mesh.devices.shape
    fine = Mesh(mesh.devices.reshape(2, src // 4, 2, dst), ("ylo", "zq", "z0", "dst"))
    rows = P(("ylo", "zq", "z0", "dst"), None)
    placed = (
        rows,
        P(),
        P(),
        P(SRC, "dst", None),
        P(SRC, "dst", None),
        P(SRC, "dst", None, None),
        P(SRC, "dst", None, None),
        rows,
    )
    return jax.shard_map(
        body, mesh=fine, in_specs=placed, out_specs=(rows, rows, P(), P()), check_vma=False
    )
```

```python
import math

import jax
import jax.numpy as jnp
from jax import lax
from jax.experimental import pallas as pl
from jax.experimental.pallas import tpu as pltpu
from jax.sharding import Mesh, PartitionSpec as P

TILE = 128
BF16 = jnp.bfloat16
F32 = jnp.float32
NN = (((1,), (0,)), ((), ()))
NT = (((1,), (1,)), ((), ()))
TN = (((0,), (0,)), ((), ()))
SRC = ("ylo", "zq", "z0")
DST = ("x", "d0")
NEAR = ("ylo", "z0")
FAR = "zq"
UNROLL = 8


def dot(a, b, dims=NN):
    return lax.dot_general(a, b, dims, preferred_element_type=F32)


def build_kernel(count_ref, pos_ref, weight_ref, tile_ref, pos_pairs, weight_pairs, *, backward):
    edges, slots = pos_ref.shape
    pairs = slots // 2
    positions = pos_ref[...].T
    weights = weight_ref[...].astype(F32).T
    pos_pairs[...] = jnp.concatenate([positions[:pairs], positions[pairs:]], axis=1)
    weight_pairs[...] = jnp.concatenate([weights[:pairs], weights[pairs:]], axis=1)
    lane = lax.broadcasted_iota(jnp.int32, (1, 2 * edges), 1)
    second = lane >= edges
    half = jnp.where(second, TILE, 0)
    one_rows = lax.broadcasted_iota(jnp.int32, (TILE, 2 * edges), 0)
    two_rows = lax.broadcasted_iota(jnp.int32, (2 * TILE, 2 * edges), 0)

    def one_pair(i, carry):
        limit = jnp.where(second, count_ref[i + pairs] + edges, count_ref[i])
        position = pos_pairs[pl.ds(i, 1), :]
        values = jnp.where(lane < limit, weight_pairs[pl.ds(i, 1), :], 0.0)
        row = position >> 7
        col = position & (TILE - 1)
        if backward:
            left = jnp.where(one_rows == col, 1.0, 0.0).astype(BF16)
            right = jnp.where(two_rows == row + half, values, 0.0).astype(BF16)
        else:
            left = jnp.where(one_rows == row, values, 0.0).astype(BF16)
            right = jnp.where(two_rows == col + half, 1.0, 0.0).astype(BF16)
        both = dot(left, right, NT).astype(BF16)
        tile_ref[i] = both[:, :TILE]
        tile_ref[i + pairs] = both[:, TILE:]
        return carry

    lax.fori_loop(0, pairs, one_pair, 0, unroll=4)


def spread_tiles(from_ref, into_ref, tile_ref, rows_ref, sums):
    block = tile_ref.shape[0]
    base = pl.program_id(0) * block
    for start in range(0, block, UNROLL):
        found = []
        for i in range(start, start + UNROLL):
            found.append((into_ref[base + i], dot(tile_ref[i], rows_ref[from_ref[base + i]])))
        for target, value in found:
            sums[target] = sums[target] + value


def forward_kernel(from_ref, into_ref, tile_ref, rows_ref, own_ref, *rest):
    sums = rest[-1]
    far = own_ref.shape[0]
    step = pl.program_id(0)

    @pl.when(step == 0)
    def _():
        sums[...] = jnp.zeros_like(sums)

    spread_tiles(from_ref, into_ref, tile_ref, rows_ref, sums)

    @pl.when(step == pl.num_programs(0) - 1)
    def _():
        own_ref[...] = sums[:far]
        for k, out_ref in enumerate(rest[:-1]):
            out_ref[...] = sums[(k + 1) * far : (k + 2) * far].astype(BF16)


def add_kernel(own_ref, *rest):
    total = own_ref[...]
    for recv_ref in rest[:-1]:
        total = total + recv_ref[...].astype(F32)
    rest[-1][...] = total.astype(BF16)


def high_low(value):
    high = value.astype(BF16).astype(F32)
    return high, value - high


def dense_kernel(recv_ref, weight_ref, bias_ref, grad_ref, hidden_ref, send_ref, agg_ref, grad_pre_ref):
    aggregated = jnp.sum(recv_ref[...].astype(F32), axis=0).astype(BF16)
    agg_ref[...] = aggregated
    weight = weight_ref[...]
    preact = dot(aggregated, weight) + bias_ref[...]
    sigma = 1.0 / (1.0 + jnp.exp(-preact))
    hidden_ref[...] = (preact * sigma).astype(BF16)
    grad_pre = (grad_ref[...].astype(F32) * sigma * (1.0 + preact * (1.0 - sigma))).astype(BF16)
    grad_pre_ref[...] = grad_pre
    back_rows = dot(grad_pre, weight, NT).astype(BF16)
    send_ref[...] = jnp.broadcast_to(back_rows[None], send_ref.shape)


def grad_kernel(place_ref, agg_ref, grad_pre_ref, *rest):
    outs, flat = rest[:-1], rest[-1]
    grad_pre = grad_pre_ref[...]
    part = dot(agg_ref[...], grad_pre, TN)
    flat[:TILE] = part[:, :TILE]
    flat[TILE:] = part[:, TILE:]
    bias_part = jnp.sum(grad_pre.astype(F32), axis=0, keepdims=True)
    sub = lax.broadcasted_iota(jnp.int32, (8, TILE), 0)
    bias_rows = jnp.where(sub == 0, bias_part[:, :TILE], jnp.where(sub == 1, bias_part[:, TILE:], 0.0))
    split_rows(place_ref[0], flat, bias_rows, outs)


def split_rows(place, flat, bias_rows, outs):
    size = outs[0].shape[0] - 8
    for k, out_ref in enumerate(outs):
        out_ref[:size] = flat[pl.ds(pl.multiple_of((place ^ k) * size, 8), size), :]
        out_ref[size:] = bias_rows


def add_parts(parts):
    total = parts[0][...]
    for part_ref in parts[1:]:
        total = total + part_ref[...]
    return total


def regrad_kernel(place_ref, *rest):
    flat = rest[-1]
    parts, outs = rest[: (len(rest) - 1) // 2], rest[(len(rest) - 1) // 2 : -1]
    total = add_parts(parts)
    size = total.shape[0] - 8
    flat[...] = total[:size]
    split_rows(place_ref[0], flat, total[size:], outs)


def share_kernel(*rest):
    out_ref = rest[-1]
    total = add_parts(rest[:-1])
    size = total.shape[0] - 8
    rows = jnp.concatenate([total[:size], bias_tile(total[size:])], axis=0).astype(BF16)
    out_ref[...] = jnp.broadcast_to(rows[None], out_ref.shape)


def bias_tile(bias_rows):
    high, low = high_low(bias_rows)
    return high + jnp.concatenate([jnp.zeros((2, TILE), F32), low[0:2], jnp.zeros((4, TILE), F32)], axis=0)


def backward_kernel(from_ref, into_ref, tile_ref, *rest):
    near_refs, (out_ref, rows, sums) = rest[:-3], rest[-3:]
    far = near_refs[0].shape[0]
    step = pl.program_id(0)

    @pl.when(step == 0)
    def _():
        sums[...] = jnp.zeros_like(sums)
        for k, near_ref in enumerate(near_refs):
            rows[k * far : (k + 1) * far] = near_ref[...]

    spread_tiles(from_ref, into_ref, tile_ref, rows, sums)

    @pl.when(step == pl.num_programs(0) - 1)
    def _():
        out_ref[:, :TILE, :] = sums[...].astype(BF16)
        out_ref[:, TILE:, :] = jnp.zeros((out_ref.shape[0], out_ref.shape[1] - TILE, TILE), BF16)


def chunk_kernel(recv_ref, send_in_ref, send_ref, bias_ref, rows, sem, *, scale):
    total = jnp.sum(recv_ref[...].astype(F32), axis=0) * scale
    size = total.shape[0] - 8
    bias_rows = total[size : size + 2] + total[size + 2 : size + 4]
    bias_ref[:, :TILE] = bias_rows[0:1]
    bias_ref[:, TILE:] = bias_rows[1:2]
    both = jnp.concatenate(high_low(total[:size]), axis=0).astype(BF16)
    rows[...] = jnp.broadcast_to(both[None], rows.shape)
    copy = pltpu.make_async_copy(rows, send_ref.at[:, TILE : TILE + 2 * size, :], sem)
    copy.start()
    copy.wait()


def final_kernel(recv_ref, input_ref, weight_grad_ref, *, group):
    pieces = recv_ref.shape[0]
    input_ref[...] = jnp.sum(recv_ref[:, :TILE, :].astype(F32), axis=0).astype(BF16)
    size = 2 * TILE // pieces
    for d in range(pieces):
        start = ((d % group) * (pieces // group) + d // group) * size
        chunk = recv_ref[d, TILE : TILE + size, :].astype(F32) + recv_ref[d, TILE + size :, :].astype(F32)
        lane = start // TILE * TILE
        weight_grad_ref[start % TILE : start % TILE + size, lane : lane + TILE] = chunk


def vmem(n):
    return [pl.BlockSpec(memory_space=pltpu.VMEM)] * n


def smem(n):
    return [pl.BlockSpec(memory_space=pltpu.SMEM)] * n


def call(kernel, name, outs, scalars, arrays, scratch=(), **more):
    single = not isinstance(outs, tuple)
    return pl.pallas_call(
        kernel,
        out_shape=outs,
        in_specs=smem(len(scalars)) + vmem(len(arrays)),
        out_specs=vmem(1)[0] if single else tuple(vmem(len(outs))),
        scratch_shapes=list(scratch),
        compiler_params=pltpu.CompilerParams(vmem_limit_bytes=56 << 20),
        name=name,
        **more,
    )(*scalars, *arrays)


def shape(dims, dtype):
    return jax.ShapeDtypeStruct(dims, dtype)


def swap(array, step, axis):
    return lax.ppermute(array, axis, [(i, i ^ step) for i in range(lax.axis_size(axis))])


def spread(kernel, name, outs, scalars, tiles, arrays, scratch):
    whole = lambda a: pl.BlockSpec(a.shape, lambda i, n=len(a.shape): (0,) * n)
    block = 16
    return pl.pallas_call(
        kernel,
        out_shape=outs,
        grid=(tiles.shape[0] // block,),
        in_specs=smem(len(scalars))
        + [pl.BlockSpec((block, TILE, TILE), lambda i: (i, 0, 0))]
        + [whole(a) for a in arrays],
        out_specs=tuple(whole(o) for o in outs),
        scratch_shapes=scratch,
        compiler_params=pltpu.CompilerParams(
            vmem_limit_bytes=56 << 20, dimension_semantics=("arbitrary",)
        ),
        name=name,
    )(*scalars, tiles, *arrays)


def body(features, weight, bias, tile_index, edge_count, edge_pos, edge_weight, grad_out):
    near = lax.axis_size(NEAR)
    far = lax.axis_size(FAR)
    group = lax.axis_size("d0")
    src = near * far
    dst = lax.axis_size(DST)
    index = tile_index.reshape(-1)
    counts = edge_count.reshape(-1)
    slots = counts.shape[0]
    positions = edge_pos.reshape(slots, -1).T
    weights = edge_weight.reshape(slots, -1).T
    edges = positions.shape[0]
    target = index // dst
    source = index % dst
    target_near = (target // (2 * far)) * 2 + target % 2
    place = (target_near ^ lax.axis_index(NEAR)) * far + (target // 2) % far
    tile_shape = shape((slots, TILE, TILE), BF16)
    block = shape((far, TILE, TILE), BF16)
    pair_scratch = (pltpu.VMEM((slots // 2, 2 * edges), jnp.int32), pltpu.VMEM((slots // 2, 2 * edges), F32))

    def build(positions, backward):
        return call(
            lambda *refs: build_kernel(*refs, backward=backward),
            "build_back" if backward else "build_tiles",
            tile_shape, (counts,), (positions, weights), pair_scratch,
        )

    sent = jnp.broadcast_to(features[None], (dst,) + features.shape)
    source_rows = lax.all_to_all(sent, DST, 0, 0, tiled=True)
    tiles = build(positions, False)
    own, *others = spread(
        forward_kernel,
        "forward_tiles",
        (shape(block.shape, F32),) + (block,) * (near - 1),
        (source, place),
        tiles,
        (source_rows,),
        [pltpu.VMEM((src, TILE, TILE), F32)],
    )
    others = [swap(other, k + 1, NEAR) for k, other in enumerate(others)]
    near_sums = call(add_kernel, "add_near", block, (), (own, *others))
    late_positions, near_sums = lax.optimization_barrier((positions, near_sums))
    back_tiles = build(late_positions, True)
    parts = lax.all_to_all(near_sums, FAR, 0, 0, tiled=True)
    parts, back_tiles = lax.optimization_barrier((parts, back_tiles))
    hidden, send, aggregated, grad_pre = call(
        dense_kernel,
        "dense_layer",
        (
            shape(grad_out.shape, BF16),
            block,
            shape(features.shape, BF16),
            shape(grad_out.shape, BF16),
        ),
        (),
        (parts, weight, bias.reshape(1, -1), grad_out),
    )
    far_rows = lax.all_to_all(send, FAR, 0, 0, tiled=True)

    quarter = shape((2 * TILE // group + 8, TILE), F32)
    piece = shape((2 * TILE // dst + 8, TILE), F32)
    own_part, *parts = call(
        grad_kernel, "grad_parts", (quarter,) * group, (lax.axis_index("d0").reshape(1),),
        (aggregated, grad_pre), (pltpu.VMEM((2 * TILE, TILE), F32),),
    )
    parts = [swap(part, k + 1, "d0") for k, part in enumerate(parts)]
    own_part, *parts = call(
        regrad_kernel, "grad_pieces", (piece,) * (dst // group), (lax.axis_index("x").reshape(1),),
        (own_part, *parts), (pltpu.VMEM((2 * TILE // group, TILE), F32),),
    )
    parts = [swap(part, k + 1, "x") for k, part in enumerate(parts)]
    share = call(share_kernel, "grad_share", shape((src,) + piece.shape, BF16), (), (own_part, *parts))
    far_rows, share = lax.optimization_barrier((far_rows, share))

    shared = lax.all_to_all(share, SRC, 0, 0, tiled=True)
    near_rows = [far_rows] + [swap(far_rows, k, NEAR) for k in range(1, near)]
    (back_send,) = spread(
        backward_kernel,
        "backward_tiles",
        (shape((dst, TILE + 2 * (piece.shape[0] - 8), TILE), BF16),),
        (place, source),
        back_tiles,
        near_rows,
        [pltpu.VMEM((src, TILE, TILE), BF16), pltpu.VMEM((dst, TILE, TILE), F32)],
    )
    node_scale = 1.0 / math.sqrt(features.shape[0] * src * dst)
    back_send, bias_grad = pl.pallas_call(
        lambda *refs: chunk_kernel(*refs, scale=node_scale),
        out_shape=(shape(back_send.shape, BF16), shape((1, 2 * TILE), F32)),
        in_specs=vmem(1) + [pl.BlockSpec(memory_space=pl.ANY)],
        out_specs=(pl.BlockSpec(memory_space=pl.ANY), pl.BlockSpec(memory_space=pltpu.VMEM)),
        scratch_shapes=[
            pltpu.VMEM((dst, back_send.shape[1] - TILE, TILE), BF16), pltpu.SemaphoreType.DMA(())
        ],
        input_output_aliases={1: 0},
        name="grad_chunk",
    )(shared, back_send)
    received = lax.all_to_all(back_send, DST, 0, 0, tiled=True)
    input_grad, weight_grad = call(
        lambda *refs: final_kernel(*refs, group=group),
        "final_sums",
        (shape(features.shape, BF16), shape((TILE, 2 * TILE), F32)),
        (),
        (received,),
    )
    return (hidden, input_grad, weight_grad, bias_grad.reshape(-1))


def solution(mesh):
    src, dst = mesh.devices.shape
    fine = Mesh(mesh.devices.reshape(2, src // 4, 2, dst // 4, 4), SRC + DST)
    rows = P(SRC + DST, None)
    placed = (
        rows,
        P(),
        P(),
        P(SRC, DST, None),
        P(SRC, DST, None),
        P(SRC, DST, None, None),
        P(SRC, DST, None, None),
        rows,
    )
    return jax.shard_map(
        body, mesh=fine, in_specs=placed, out_specs=(rows, rows, P(), P()), check_vma=False
    )
```

```python
import math

import jax
import jax.numpy as jnp
from jax import lax
from jax.experimental import pallas as pl
from jax.experimental.pallas import tpu as pltpu
from jax.sharding import Mesh, PartitionSpec as P

TILE = 128
BF16 = jnp.bfloat16
F32 = jnp.float32
NN = (((1,), (0,)), ((), ()))
NT = (((1,), (1,)), ((), ()))
TN = (((0,), (0,)), ((), ()))
SRC = ("ylo", "zq", "z0")
NEAR = ("ylo", "z0")
FAR = "zq"
UNROLL = 8


def dot(a, b, dims=NN):
    return lax.dot_general(a, b, dims, preferred_element_type=F32)


def build_kernel(count_ref, pos_ref, weight_ref, tile_ref, pos_pairs, weight_pairs, *, backward):
    edges, slots = pos_ref.shape
    pairs = slots // 2
    positions = pos_ref[...].T
    weights = weight_ref[...].astype(F32).T
    pos_pairs[...] = jnp.concatenate([positions[:pairs], positions[pairs:]], axis=1)
    weight_pairs[...] = jnp.concatenate([weights[:pairs], weights[pairs:]], axis=1)
    lane = lax.broadcasted_iota(jnp.int32, (1, 2 * edges), 1)
    second = lane >= edges
    half = jnp.where(second, TILE, 0)
    one_rows = lax.broadcasted_iota(jnp.int32, (TILE, 2 * edges), 0)
    two_rows = lax.broadcasted_iota(jnp.int32, (2 * TILE, 2 * edges), 0)

    def one_pair(i, carry):
        limit = jnp.where(second, count_ref[i + pairs] + edges, count_ref[i])
        position = pos_pairs[pl.ds(i, 1), :]
        values = jnp.where(lane < limit, weight_pairs[pl.ds(i, 1), :], 0.0)
        row = position >> 7
        col = position & (TILE - 1)
        if backward:
            left = jnp.where(one_rows == col, 1.0, 0.0).astype(BF16)
            right = jnp.where(two_rows == row + half, values, 0.0).astype(BF16)
        else:
            left = jnp.where(one_rows == row, values, 0.0).astype(BF16)
            right = jnp.where(two_rows == col + half, 1.0, 0.0).astype(BF16)
        both = dot(left, right, NT).astype(BF16)
        tile_ref[i] = both[:, :TILE]
        tile_ref[i + pairs] = both[:, TILE:]
        return carry

    lax.fori_loop(0, pairs, one_pair, 0, unroll=4)


def spread_tiles(from_ref, into_ref, tile_ref, rows_ref, sums):
    sums[...] = jnp.zeros_like(sums)

    def one_step(step, carry):
        found = []
        for j in range(UNROLL):
            i = step * UNROLL + j
            found.append((into_ref[i], dot(tile_ref[i], rows_ref[from_ref[i]])))
        for target, value in found:
            sums[target] = sums[target] + value
        return carry

    lax.fori_loop(0, tile_ref.shape[0] // UNROLL, one_step, 0)


def forward_kernel(from_ref, into_ref, tile_ref, rows_ref, out_ref, sums):
    spread_tiles(from_ref, into_ref, tile_ref, rows_ref, sums)
    out_ref[...] = sums[...].astype(BF16)


def high_low(value):
    high = value.astype(BF16).astype(F32)
    return high, value - high


def bias_tile(bias_rows):
    high, low = high_low(bias_rows[0:2])
    return jnp.concatenate([high, low, jnp.zeros((4, TILE), F32)], axis=0).astype(BF16)


def bias_sum(tile):
    return tile[0:2] + tile[2:4]


def dense_kernel(recv_ref, weight_ref, bias_ref, grad_ref, hidden_ref, send_ref):
    peers = recv_ref.shape[0]
    aggregated = jnp.sum(recv_ref[...].astype(F32), axis=0).astype(BF16)
    weight = weight_ref[...]
    preact = dot(aggregated, weight) + bias_ref[...]
    sigma = 1.0 / (1.0 + jnp.exp(-preact))
    hidden_ref[...] = (preact * sigma).astype(BF16)
    grad_pre = (grad_ref[...].astype(F32) * sigma * (1.0 + preact * (1.0 - sigma))).astype(BF16)
    back_rows = dot(grad_pre, weight, NT).astype(BF16)
    send_ref[:, :TILE, :] = jnp.broadcast_to(back_rows[None], (peers, TILE, TILE))
    part = dot(aggregated, grad_pre, TN).astype(BF16)
    rows = TILE // peers
    send_ref[:, TILE : TILE + rows, :] = part[:, :TILE].reshape(peers, rows, TILE)
    send_ref[:, TILE + rows : TILE + 2 * rows, :] = part[:, TILE:].reshape(peers, rows, TILE)
    bias_part = jnp.sum(grad_pre.astype(F32), axis=0, keepdims=True)
    bias_rows = jnp.concatenate([bias_part[:, :TILE], bias_part[:, TILE:]], axis=0)
    send_ref[:, TILE + 2 * rows :, :] = jnp.broadcast_to(bias_tile(bias_rows)[None], (peers, 8, TILE))


def middle_kernel(recv_ref, out_ref):
    peers = recv_ref.shape[0]
    top = peers * TILE
    out_ref[:top] = recv_ref[:, :TILE, :].reshape(top, TILE)
    total = jnp.sum(recv_ref[:, TILE:, :].astype(F32), axis=0)
    rows = total.shape[0] - 8
    high, low = high_low(total[:rows])
    out_ref[top : top + rows] = high.astype(BF16)
    out_ref[top + rows : top + 2 * rows] = low.astype(BF16)
    out_ref[top + 2 * rows :] = bias_tile(bias_sum(total[rows:]))


def share_kernel(*rest):
    extra_refs, out_ref = rest[:-1], rest[-1]
    total = extra_refs[0][...].astype(F32)
    for extra_ref in extra_refs[1:]:
        total = total + extra_ref[...].astype(F32)
    rows = (total.shape[0] - 8) // 2
    chunk = (total[:rows] + total[rows : 2 * rows]).astype(BF16)
    out_ref[:, :rows, :] = jnp.broadcast_to(chunk[None], (out_ref.shape[0], rows, TILE))
    tile = bias_tile(bias_sum(total[2 * rows :]))
    out_ref[:, rows:, :] = jnp.broadcast_to(tile[None], (out_ref.shape[0], 8, TILE))


def chunk_kernel(recv_ref, chunk_ref, bias_grad_ref, *, scale):
    total = jnp.sum(recv_ref[...].astype(F32), axis=0) * scale
    rows = total.shape[0] - 8
    chunk_ref[...] = total[:rows]
    bias_rows = bias_sum(total[rows:])
    bias_grad_ref[:, :TILE] = bias_rows[0:1]
    bias_grad_ref[:, TILE:] = bias_rows[1:2]


def backward_kernel(from_ref, into_ref, tile_ref, *rest):
    near_refs, (out_ref, rows, sums) = rest[:-3], rest[-3:]
    far = rows.shape[0] // len(near_refs)
    top = far * TILE
    for k, near_ref in enumerate(near_refs):
        rows[k * far : (k + 1) * far] = near_ref[:top].reshape(far, TILE, TILE)
    spread_tiles(from_ref, into_ref, tile_ref, rows, sums)
    out_ref[...] = sums[...].astype(BF16)


def weight_kernel(own_ref, *rest):
    pair_refs, out_ref = rest[:-1], rest[-1]
    rows = pair_refs[0].shape[1]
    half = rows // 2
    for k, pair_ref in enumerate(pair_refs):
        for j in range(2):
            start = pl.multiple_of((own_ref[0] ^ (2 * k + j)) * half, 8)
            out_ref[pl.ds(start, half), :TILE] = pair_ref[j, :half, :]
            out_ref[pl.ds(start, half), TILE:] = pair_ref[j, half:, :]


def vmem(n):
    return [pl.BlockSpec(memory_space=pltpu.VMEM)] * n


def smem(n):
    return [pl.BlockSpec(memory_space=pltpu.SMEM)] * n


def call(kernel, name, outs, scalars, arrays, scratch=(), **more):
    single = not isinstance(outs, tuple)
    return pl.pallas_call(
        kernel,
        out_shape=outs,
        in_specs=smem(len(scalars)) + vmem(len(arrays)),
        out_specs=vmem(1)[0] if single else tuple(vmem(len(outs))),
        scratch_shapes=list(scratch),
        compiler_params=pltpu.CompilerParams(vmem_limit_bytes=56 << 20),
        name=name,
        **more,
    )(*scalars, *arrays)


def shape(dims, dtype):
    return jax.ShapeDtypeStruct(dims, dtype)


def swap(array, step, axis):
    return lax.ppermute(array, axis, [(i, i ^ step) for i in range(lax.axis_size(axis))])


def body(features, weight, bias, tile_index, edge_count, edge_pos, edge_weight, grad_out):
    near = lax.axis_size(NEAR)
    far = lax.axis_size(FAR)
    src = near * far
    dst = lax.axis_size("dst")
    index = tile_index.reshape(-1)
    counts = edge_count.reshape(-1)
    slots = counts.shape[0]
    positions = edge_pos.reshape(slots, -1).T
    weights = edge_weight.reshape(slots, -1).T
    edges = positions.shape[0]
    target = index // dst
    source = index % dst
    target_near = (target // (2 * far)) * 2 + target % 2
    target_far = (target // 2) % far
    place = target_near * far + target_far
    back_place = (target_near ^ lax.axis_index(NEAR)) * far + target_far
    tile_shape = shape((slots, TILE, TILE), BF16)
    block = shape((far, TILE, TILE), BF16)
    pair_scratch = (pltpu.VMEM((slots // 2, 2 * edges), jnp.int32), pltpu.VMEM((slots // 2, 2 * edges), F32))

    def build(positions, backward):
        return call(
            lambda *refs: build_kernel(*refs, backward=backward),
            "build_back" if backward else "build_tiles",
            tile_shape, (counts,), (positions, weights), pair_scratch,
        )

    sent = jnp.broadcast_to(features[None], (dst,) + features.shape)
    source_rows = lax.all_to_all(sent, "dst", 0, 0, tiled=True)
    tiles = build(positions, False)
    partial = call(
        forward_kernel, "forward_tiles", shape((src, TILE, TILE), BF16), (source, place),
        (tiles, source_rows), (pltpu.VMEM((src, TILE, TILE), F32),),
    )
    near_parts = lax.all_to_all(partial.reshape(near, far, TILE, TILE), NEAR, 0, 0, tiled=True)
    late_positions, partial = lax.optimization_barrier((positions, partial))
    back_tiles = build(late_positions, True)
    near_sums = jnp.sum(near_parts.astype(F32), axis=0).astype(BF16)
    near_sums, back_tiles = lax.optimization_barrier((near_sums, back_tiles))
    parts = lax.all_to_all(near_sums, FAR, 0, 0, tiled=True)
    rows = 2 * TILE // far
    hidden, send = call(
        dense_kernel,
        "dense_layer",
        (shape(grad_out.shape, BF16), shape((far, TILE + rows + 8, TILE), BF16)),
        (),
        (parts, weight, bias.reshape(1, -1), grad_out),
    )
    far_rows = lax.all_to_all(send, FAR, 0, 0, tiled=True)
    top = far * TILE
    near_rows = call(
        middle_kernel, "middle_sums", shape((top + 2 * rows + 8, TILE), BF16), (), (far_rows,)
    )
    near_all = [near_rows] + [swap(near_rows, k, NEAR) for k in range(1, near)]
    share = call(
        share_kernel, "grad_share", shape((dst, rows + 8, TILE), BF16), (), [part[top:] for part in near_all]
    )
    shared = lax.all_to_all(share, "dst", 0, 0, tiled=True)
    back_send = call(
        backward_kernel,
        "backward_tiles",
        shape((dst, TILE, TILE), BF16),
        (back_place, source),
        (back_tiles, *near_all),
        (pltpu.VMEM((src, TILE, TILE), BF16), pltpu.VMEM((dst, TILE, TILE), F32)),
    )
    shared, back_send = lax.optimization_barrier((shared, back_send))
    received = lax.all_to_all(back_send, "dst", 0, 0, tiled=True)
    node_scale = 1.0 / math.sqrt(features.shape[0] * src * dst)
    chunk, bias_grad = call(
        lambda *refs: chunk_kernel(*refs, scale=node_scale),
        "grad_chunk",
        (shape((rows, TILE), F32), shape((1, 2 * TILE), F32)),
        (),
        (shared,),
    )
    pair = jnp.stack([chunk, swap(chunk, 1, FAR)])
    pairs = [pair] + [swap(pair, k, FAR) for k in range(2, far, 2)]
    weight_grad = call(
        weight_kernel, "weight_rows", shape((TILE, 2 * TILE), F32), (lax.axis_index(FAR).reshape(1),), pairs
    )
    input_grad = jnp.sum(received.astype(F32), axis=0).astype(BF16)
    return (hidden, input_grad, weight_grad, bias_grad.reshape(-1))


def solution(mesh):
    src, dst = mesh.devices.shape
    fine = Mesh(mesh.devices.reshape(2, src // 4, 2, dst), ("ylo", "zq", "z0", "dst"))
    rows = P(("ylo", "zq", "z0", "dst"), None)
    placed = (
        rows,
        P(),
        P(),
        P(SRC, "dst", None),
        P(SRC, "dst", None),
        P(SRC, "dst", None, None),
        P(SRC, "dst", None, None),
        rows,
    )
    return jax.shard_map(
        body, mesh=fine, in_specs=placed, out_specs=(rows, rows, P(), P()), check_vma=False
    )
```

```python
import math

import jax
import jax.numpy as jnp
from jax import lax
from jax.experimental import pallas as pl
from jax.experimental.pallas import tpu as pltpu
from jax.sharding import Mesh, PartitionSpec as P

TILE = 128
BF16 = jnp.bfloat16
F32 = jnp.float32
NN = (((1,), (0,)), ((), ()))
NT = (((1,), (1,)), ((), ()))
TN = (((0,), (0,)), ((), ()))
SRC = ("ylo", "zq", "z0")
NEAR = ("ylo", "z0")
FAR = "zq"
GROUP = 16
BLOCKS = 2


def dot(a, b, dims=NN):
    return lax.dot_general(a, b, dims, preferred_element_type=F32)


def build_kernel(count_ref, pos_ref, weight_ref, tile_ref, pos_pairs, weight_pairs, *, backward):
    edges, slots = pos_ref.shape
    pairs = slots // 2
    positions = pos_ref[...].T
    weights = weight_ref[...].astype(F32).T
    pos_pairs[...] = jnp.concatenate([positions[:pairs], positions[pairs:]], axis=1)
    weight_pairs[...] = jnp.concatenate([weights[:pairs], weights[pairs:]], axis=1)
    lane = lax.broadcasted_iota(jnp.int32, (1, 2 * edges), 1)
    second = lane >= edges
    half = jnp.where(second, TILE, 0)
    one_rows = lax.broadcasted_iota(jnp.int32, (TILE, 2 * edges), 0)
    two_rows = lax.broadcasted_iota(jnp.int32, (2 * TILE, 2 * edges), 0)

    def one_pair(i, carry):
        limit = jnp.where(second, count_ref[i + pairs] + edges, count_ref[i])
        position = pos_pairs[pl.ds(i, 1), :]
        values = jnp.where(lane < limit, weight_pairs[pl.ds(i, 1), :], 0.0)
        row = position >> 7
        col = position & (TILE - 1)
        if backward:
            left = jnp.where(one_rows == col, 1.0, 0.0).astype(BF16)
            right = jnp.where(two_rows == row + half, values, 0.0).astype(BF16)
        else:
            left = jnp.where(one_rows == row, values, 0.0).astype(BF16)
            right = jnp.where(two_rows == col + half, 1.0, 0.0).astype(BF16)
        both = dot(left, right, NT).astype(BF16)
        tile_ref[i] = both[:, :TILE]
        tile_ref[i + pairs] = both[:, TILE:]
        return carry

    lax.fori_loop(0, pairs, one_pair, 0, unroll=4)


def spread_tiles(index_ref, tile_ref, rows_ref, sums, split, backward):
    block = tile_ref.shape[0]
    step = pl.program_id(0)
    shift = split.bit_length() - 1
    for start in range(0, block, GROUP):
        found = []
        for i in range(start, start + GROUP):
            index = index_ref[step * block + i]
            target = index >> shift
            source = index & (split - 1)
            if backward:
                found.append((source, dot(tile_ref[i], rows_ref[target])))
            else:
                found.append((target, dot(tile_ref[i], rows_ref[source])))
        for place, value in found:
            sums[place] = sums[place] + value


def forward_kernel(index_ref, tile_ref, rows_ref, out_ref, sums):
    near, far = out_ref.shape[:2]
    step = pl.program_id(0)

    @pl.when(step == 0)
    def _():
        sums[...] = jnp.zeros_like(sums)

    spread_tiles(index_ref, tile_ref, rows_ref, sums, rows_ref.shape[0], False)

    @pl.when(step == pl.num_programs(0) - 1)
    def _():
        for target in range(sums.shape[0]):
            place = target // (2 * far) * 2 + target % 2
            out_ref[place, target // 2 % far] = sums[target].astype(BF16)


def high_low(value):
    high = value.astype(BF16).astype(F32)
    return high, value - high


def bias_tile(bias_rows):
    high, low = high_low(bias_rows[0:2])
    return jnp.concatenate([high, low, jnp.zeros((4, TILE), F32)], axis=0).astype(BF16)


def bias_sum(tile):
    return tile[0:2] + tile[2:4]


def dense_kernel(agg_ref, weight_ref, bias_ref, grad_ref, hidden_ref, send_ref):
    peers = send_ref.shape[0]
    aggregated = agg_ref[...]
    weight = weight_ref[...]
    preact = dot(aggregated, weight) + bias_ref[...]
    sigma = 1.0 / (1.0 + jnp.exp(-preact))
    hidden_ref[...] = (preact * sigma).astype(BF16)
    grad_pre = (grad_ref[...].astype(F32) * sigma * (1.0 + preact * (1.0 - sigma))).astype(BF16)
    back_rows = dot(grad_pre, weight, NT).astype(BF16)
    send_ref[:, :TILE, :] = jnp.broadcast_to(back_rows[None], (peers, TILE, TILE))
    part = dot(aggregated, grad_pre, TN).astype(BF16)
    rows = TILE // peers
    send_ref[:, TILE : TILE + rows, :] = part[:, :TILE].reshape(peers, rows, TILE)
    send_ref[:, TILE + rows : TILE + 2 * rows, :] = part[:, TILE:].reshape(peers, rows, TILE)
    bias_part = jnp.sum(grad_pre.astype(F32), axis=0, keepdims=True)
    bias_rows = jnp.concatenate([bias_part[:, :TILE], bias_part[:, TILE:]], axis=0)
    send_ref[:, TILE + 2 * rows :, :] = jnp.broadcast_to(bias_tile(bias_rows)[None], (peers, 8, TILE))


def middle_kernel(recv_ref, out_ref):
    near = out_ref.shape[0]
    peers = recv_ref.shape[0]
    top = peers * TILE
    back_rows = recv_ref[:, :TILE, :].reshape(top, TILE)
    total = jnp.sum(recv_ref[:, TILE:, :].astype(F32), axis=0)
    rows = total.shape[0] - 8
    high, low = high_low(total[:rows])
    tile = bias_tile(bias_sum(total[rows:]))
    extra = jnp.concatenate([high.astype(BF16), low.astype(BF16), tile], axis=0)
    for k in range(near):
        out_ref[k, :top] = back_rows
        out_ref[k, top:] = extra


def backward_kernel(index_ref, tile_ref, recv_ref, out_ref, rows, sums):
    near = recv_ref.shape[0]
    far = rows.shape[0] // near
    top = far * TILE
    pieces = out_ref.shape[0]
    step = pl.program_id(0)

    @pl.when(step == 0)
    def _():
        sums[...] = jnp.zeros_like(sums)
        for target in range(near * far):
            start = target // 2 % far * TILE
            rows[target] = recv_ref[target // (2 * far) * 2 + target % 2, start : start + TILE]

    spread_tiles(index_ref, tile_ref, rows, sums, pieces, True)

    @pl.when(step == pl.num_programs(0) - 1)
    def _():
        out_ref[:, :TILE, :] = sums[...].astype(BF16)
        total = jnp.sum(recv_ref[:, top:, :].astype(F32), axis=0)
        count = (total.shape[0] - 8) // 2
        chunk = (total[:count] + total[count : 2 * count]).astype(BF16)
        out_ref[:, TILE : TILE + count, :] = jnp.broadcast_to(chunk[None], (pieces, count, TILE))
        tile = bias_tile(bias_sum(total[2 * count :]))
        out_ref[:, TILE + count :, :] = jnp.broadcast_to(tile[None], (pieces, 8, TILE))


def vmem(n):
    return [pl.BlockSpec(memory_space=pltpu.VMEM)] * n


def smem(n):
    return [pl.BlockSpec(memory_space=pltpu.SMEM)] * n


def call(kernel, name, outs, scalars, arrays, scratch=(), **more):
    single = not isinstance(outs, tuple)
    return pl.pallas_call(
        kernel,
        out_shape=outs,
        in_specs=smem(len(scalars)) + vmem(len(arrays)),
        out_specs=vmem(1)[0] if single else tuple(vmem(len(outs))),
        scratch_shapes=list(scratch),
        compiler_params=pltpu.CompilerParams(vmem_limit_bytes=56 << 20),
        name=name,
        **more,
    )(*scalars, *arrays)


def shape(dims, dtype):
    return jax.ShapeDtypeStruct(dims, dtype)


def spread(kernel, name, out, index, tiles, rows, scratch):
    whole = lambda a: pl.BlockSpec(a.shape, lambda i, n=len(a.shape): (0,) * n)
    block = tiles.shape[0] // BLOCKS
    return pl.pallas_call(
        kernel,
        out_shape=out,
        grid=(BLOCKS,),
        in_specs=smem(1) + [pl.BlockSpec((block, TILE, TILE), lambda i: (i, 0, 0)), whole(rows)],
        out_specs=whole(out),
        scratch_shapes=scratch,
        compiler_params=pltpu.CompilerParams(
            vmem_limit_bytes=56 << 20, dimension_semantics=("arbitrary",)
        ),
        name=name,
    )(index, tiles, rows)


def body(features, weight, bias, tile_index, edge_count, edge_pos, edge_weight, grad_out):
    near = lax.axis_size(NEAR)
    far = lax.axis_size(FAR)
    src = near * far
    dst = lax.axis_size("dst")
    index = tile_index.reshape(-1)
    counts = edge_count.reshape(-1)
    slots = counts.shape[0]
    positions = edge_pos.reshape(slots, -1).T
    weights = edge_weight.reshape(slots, -1).T
    edges = positions.shape[0]
    tile_shape = shape((slots, TILE, TILE), BF16)
    pair_scratch = (pltpu.VMEM((slots // 2, 2 * edges), jnp.int32), pltpu.VMEM((slots // 2, 2 * edges), F32))

    def build(positions, backward):
        return call(
            lambda *refs: build_kernel(*refs, backward=backward),
            "build_back" if backward else "build_tiles",
            tile_shape, (counts,), (positions, weights), pair_scratch,
        )

    sent = jnp.broadcast_to(features[None], (dst,) + features.shape)
    source_rows = lax.all_to_all(sent, "dst", 0, 0, tiled=True)
    tiles = build(positions, False)
    partial = spread(
        forward_kernel, "forward_tiles", shape((near, far, TILE, TILE), BF16),
        index, tiles, source_rows, [pltpu.VMEM((src, TILE, TILE), F32)],
    )
    near_parts = lax.all_to_all(partial, NEAR, 0, 0, tiled=True)
    late_positions, partial = lax.optimization_barrier((positions, partial))
    back_tiles = build(late_positions, True)
    near_sums = jnp.sum(near_parts.astype(F32), axis=0).astype(BF16)
    near_sums, back_tiles = lax.optimization_barrier((near_sums, back_tiles))
    parts = lax.all_to_all(near_sums, FAR, 0, 0, tiled=True)
    aggregated = jnp.sum(parts.astype(F32), axis=0).astype(BF16)
    rows = 2 * TILE // far
    hidden, send = call(
        dense_kernel,
        "dense_layer",
        (shape(grad_out.shape, BF16), shape((far, TILE + rows + 8, TILE), BF16)),
        (),
        (aggregated, weight, bias.reshape(1, -1), grad_out),
    )
    far_rows = lax.all_to_all(send, FAR, 0, 0, tiled=True)
    near_rows = call(
        middle_kernel, "middle_sums", shape((near, far * TILE + 2 * rows + 8, TILE), BF16), (), (far_rows,)
    )
    near_rows = lax.all_to_all(near_rows, NEAR, 0, 0, tiled=True)
    back_send = spread(
        backward_kernel, "backward_tiles", shape((dst, TILE + rows + 8, TILE), BF16),
        index, back_tiles, near_rows,
        [pltpu.VMEM((src, TILE, TILE), BF16), pltpu.VMEM((dst, TILE, TILE), F32)],
    )
    received = lax.all_to_all(back_send, "dst", 0, 0, tiled=True)
    node_scale = 1.0 / math.sqrt(features.shape[0] * src * dst)
    extra = jnp.sum(received[:, TILE:, :].astype(F32), axis=0) * node_scale
    chunk = jnp.concatenate([extra[: rows // 2], extra[rows // 2 : rows]], axis=1).astype(BF16)
    chunks = lax.all_to_all(jnp.broadcast_to(chunk[None], (far,) + chunk.shape), FAR, 0, 0, tiled=True)
    weight_grad = chunks.reshape(TILE, 2 * TILE).astype(F32)
    bias_grad = bias_sum(extra[rows:]).reshape(-1)
    input_grad = jnp.sum(received[:, :TILE, :].astype(F32), axis=0).astype(BF16)
    return (hidden, input_grad, weight_grad, bias_grad)


def solution(mesh):
    src, dst = mesh.devices.shape
    fine = Mesh(mesh.devices.reshape(2, src // 4, 2, dst), ("ylo", "zq", "z0", "dst"))
    rows = P(("ylo", "zq", "z0", "dst"), None)
    placed = (
        rows,
        P(),
        P(),
        P(SRC, "dst", None),
        P(SRC, "dst", None),
        P(SRC, "dst", None, None),
        P(SRC, "dst", None, None),
        rows,
    )
    return jax.shard_map(
        body, mesh=fine, in_specs=placed, out_specs=(rows, rows, P(), P()), check_vma=False
    )
```

```python
import math

import jax
import jax.numpy as jnp
from jax import lax
from jax.experimental import pallas as pl
from jax.experimental.pallas import tpu as pltpu
from jax.sharding import Mesh, PartitionSpec as P

TILE = 128
BF16 = jnp.bfloat16
F32 = jnp.float32
NN = (((1,), (0,)), ((), ()))
NT = (((1,), (1,)), ((), ()))
TN = (((0,), (0,)), ((), ()))
SRC = ("ylo", "zq", "z0")
NEAR = ("ylo", "z0")
FAR = "zq"
GROUP = 32


def dot(a, b, dims=NN):
    return lax.dot_general(a, b, dims, preferred_element_type=F32)


def build_kernel(count_ref, pos_ref, weight_ref, tile_ref, pos_pairs, weight_pairs, *, backward):
    edges, slots = pos_ref.shape
    pairs = slots // 2
    positions = pos_ref[...].T
    weights = weight_ref[...].astype(F32).T
    pos_pairs[...] = jnp.concatenate([positions[:pairs], positions[pairs:]], axis=1)
    weight_pairs[...] = jnp.concatenate([weights[:pairs], weights[pairs:]], axis=1)
    lane = lax.broadcasted_iota(jnp.int32, (1, 2 * edges), 1)
    second = lane >= edges
    half = jnp.where(second, TILE, 0)
    one_rows = lax.broadcasted_iota(jnp.int32, (TILE, 2 * edges), 0)
    two_rows = lax.broadcasted_iota(jnp.int32, (2 * TILE, 2 * edges), 0)

    def one_pair(i, carry):
        limit = jnp.where(second, count_ref[i + pairs] + edges, count_ref[i])
        position = pos_pairs[pl.ds(i, 1), :]
        values = jnp.where(lane < limit, weight_pairs[pl.ds(i, 1), :], 0.0)
        row = position >> 7
        col = position & (TILE - 1)
        if backward:
            left = jnp.where(one_rows == col, 1.0, 0.0).astype(BF16)
            right = jnp.where(two_rows == row + half, values, 0.0).astype(BF16)
        else:
            left = jnp.where(one_rows == row, values, 0.0).astype(BF16)
            right = jnp.where(two_rows == col + half, 1.0, 0.0).astype(BF16)
        both = dot(left, right, NT).astype(BF16)
        tile_ref[i] = both[:, :TILE]
        tile_ref[i + pairs] = both[:, TILE:]
        return carry

    lax.fori_loop(0, pairs, one_pair, 0, unroll=4)


def spread_tiles(index_ref, tile_ref, rows_ref, sums, split, backward):
    shift = split.bit_length() - 1
    sums[...] = jnp.zeros_like(sums)

    def one_step(step, carry):
        found = []
        for i in range(GROUP):
            slot = step * GROUP + i
            index = index_ref[slot]
            target = index >> shift
            source = index & (split - 1)
            if backward:
                found.append((source, dot(tile_ref[slot], rows_ref[target])))
            else:
                found.append((target, dot(tile_ref[slot], rows_ref[source])))
        for place, value in found:
            sums[place] = sums[place] + value
        return carry

    lax.fori_loop(0, tile_ref.shape[0] // GROUP, one_step, 0)


def forward_kernel(index_ref, tile_ref, rows_ref, out_ref, sums):
    near, far = out_ref.shape[:2]
    spread_tiles(index_ref, tile_ref, rows_ref, sums, rows_ref.shape[0], False)
    for target in range(near * far):
        place = target // (2 * far) * 2 + target % 2
        out_ref[place, target // 2 % far] = sums[target].astype(BF16)


def high_low(value):
    high = value.astype(BF16).astype(F32)
    return high, value - high


def bias_tile(bias_rows):
    high, low = high_low(bias_rows[0:2])
    return jnp.concatenate([high, low, jnp.zeros((4, TILE), F32)], axis=0).astype(BF16)


def bias_sum(tile):
    return tile[0:2] + tile[2:4]


def dense_kernel(agg_ref, weight_ref, bias_ref, grad_ref, hidden_ref, send_ref):
    peers = send_ref.shape[0]
    aggregated = agg_ref[...]
    weight = weight_ref[...]
    preact = dot(aggregated, weight) + bias_ref[...]
    sigma = 1.0 / (1.0 + jnp.exp(-preact))
    hidden_ref[...] = (preact * sigma).astype(BF16)
    grad_pre = (grad_ref[...].astype(F32) * sigma * (1.0 + preact * (1.0 - sigma))).astype(BF16)
    back_rows = dot(grad_pre, weight, NT).astype(BF16)
    send_ref[:, :TILE, :] = jnp.broadcast_to(back_rows[None], (peers, TILE, TILE))
    part = dot(aggregated, grad_pre, TN).astype(BF16)
    rows = TILE // peers
    send_ref[:, TILE : TILE + rows, :] = part[:, :TILE].reshape(peers, rows, TILE)
    send_ref[:, TILE + rows : TILE + 2 * rows, :] = part[:, TILE:].reshape(peers, rows, TILE)
    bias_part = jnp.sum(grad_pre.astype(F32), axis=0, keepdims=True)
    bias_rows = jnp.concatenate([bias_part[:, :TILE], bias_part[:, TILE:]], axis=0)
    send_ref[:, TILE + 2 * rows :, :] = jnp.broadcast_to(bias_tile(bias_rows)[None], (peers, 8, TILE))


def middle_kernel(recv_ref, out_ref):
    near = out_ref.shape[0]
    peers = recv_ref.shape[0]
    top = peers * TILE
    back_rows = recv_ref[:, :TILE, :].reshape(top, TILE)
    total = jnp.sum(recv_ref[:, TILE:, :].astype(F32), axis=0)
    rows = total.shape[0] - 8
    high, low = high_low(total[:rows])
    tile = bias_tile(bias_sum(total[rows:]))
    extra = jnp.concatenate([high.astype(BF16), low.astype(BF16), tile], axis=0)
    for k in range(near):
        out_ref[k, :top] = back_rows
        out_ref[k, top:] = extra


def backward_kernel(index_ref, tile_ref, recv_ref, out_ref, rows, sums):
    near = recv_ref.shape[0]
    far = rows.shape[0] // near
    top = far * TILE
    pieces = out_ref.shape[0]
    for target in range(near * far):
        start = target // 2 % far * TILE
        rows[target] = recv_ref[target // (2 * far) * 2 + target % 2, start : start + TILE]
    spread_tiles(index_ref, tile_ref, rows, sums, pieces, True)
    out_ref[:, :TILE, :] = sums[...].astype(BF16)
    total = jnp.sum(recv_ref[:, top:, :].astype(F32), axis=0)
    count = (total.shape[0] - 8) // 2
    chunk = (total[:count] + total[count : 2 * count]).astype(BF16)
    out_ref[:, TILE : TILE + count, :] = jnp.broadcast_to(chunk[None], (pieces, count, TILE))
    tile = bias_tile(bias_sum(total[2 * count :]))
    out_ref[:, TILE + count :, :] = jnp.broadcast_to(tile[None], (pieces, 8, TILE))


def vmem(n):
    return [pl.BlockSpec(memory_space=pltpu.VMEM)] * n


def smem(n):
    return [pl.BlockSpec(memory_space=pltpu.SMEM)] * n


def call(kernel, name, outs, scalars, arrays, scratch=(), **more):
    single = not isinstance(outs, tuple)
    return pl.pallas_call(
        kernel,
        out_shape=outs,
        in_specs=smem(len(scalars)) + vmem(len(arrays)),
        out_specs=vmem(1)[0] if single else tuple(vmem(len(outs))),
        scratch_shapes=list(scratch),
        compiler_params=pltpu.CompilerParams(vmem_limit_bytes=20 << 20),
        name=name,
        **more,
    )(*scalars, *arrays)


def shape(dims, dtype):
    return jax.ShapeDtypeStruct(dims, dtype)


def body(features, weight, bias, tile_index, edge_count, edge_pos, edge_weight, grad_out):
    near = lax.axis_size(NEAR)
    far = lax.axis_size(FAR)
    src = near * far
    dst = lax.axis_size("dst")
    index = tile_index.reshape(-1)
    counts = edge_count.reshape(-1)
    slots = counts.shape[0]
    positions = edge_pos.reshape(slots, -1).T
    weights = edge_weight.reshape(slots, -1).T
    edges = positions.shape[0]
    tile_shape = shape((slots, TILE, TILE), BF16)
    pair_scratch = (pltpu.VMEM((slots // 2, 2 * edges), jnp.int32), pltpu.VMEM((slots // 2, 2 * edges), F32))

    def build(positions, backward):
        return call(
            lambda *refs: build_kernel(*refs, backward=backward),
            "build_back" if backward else "build_tiles",
            tile_shape, (counts,), (positions, weights), pair_scratch,
        )

    sent = jnp.broadcast_to(features[None], (dst,) + features.shape)
    source_rows = lax.all_to_all(sent, "dst", 0, 0, tiled=True)
    tiles = build(positions, False)
    partial = call(
        forward_kernel, "forward_tiles", shape((near, far, TILE, TILE), BF16),
        (index,), (tiles, source_rows), [pltpu.VMEM((src, TILE, TILE), F32)],
    )
    near_parts = lax.all_to_all(partial, NEAR, 0, 0, tiled=True)
    near_sums = jnp.sum(near_parts.astype(F32), axis=0).astype(BF16)
    late_positions, near_sums = lax.optimization_barrier((positions, near_sums))
    back_tiles = build(late_positions, True)
    parts = lax.all_to_all(near_sums, FAR, 0, 0, tiled=True)
    parts, back_tiles = lax.optimization_barrier((parts, back_tiles))
    aggregated = jnp.sum(parts.astype(F32), axis=0).astype(BF16)
    rows = 2 * TILE // far
    hidden, send = call(
        dense_kernel,
        "dense_layer",
        (shape(grad_out.shape, BF16), shape((far, TILE + rows + 8, TILE), BF16)),
        (),
        (aggregated, weight, bias.reshape(1, -1), grad_out),
    )
    far_rows = lax.all_to_all(send, FAR, 0, 0, tiled=True)
    near_rows = call(
        middle_kernel, "middle_sums", shape((near, far * TILE + 2 * rows + 8, TILE), BF16), (), (far_rows,)
    )
    near_rows = lax.all_to_all(near_rows, NEAR, 0, 0, tiled=True)
    back_send = call(
        backward_kernel, "backward_tiles", shape((dst, TILE + rows + 8, TILE), BF16),
        (index,), (back_tiles, near_rows),
        [pltpu.VMEM((src, TILE, TILE), BF16), pltpu.VMEM((dst, TILE, TILE), F32)],
    )
    received = lax.all_to_all(back_send, "dst", 0, 0, tiled=True)
    node_scale = 1.0 / math.sqrt(features.shape[0] * src * dst)
    extra = jnp.sum(received[:, TILE:, :].astype(F32), axis=0) * node_scale
    chunk = jnp.concatenate([extra[: rows // 2], extra[rows // 2 : rows]], axis=1).astype(BF16)
    chunks = lax.all_to_all(jnp.broadcast_to(chunk[None], (far,) + chunk.shape), FAR, 0, 0, tiled=True)
    weight_grad = chunks.reshape(TILE, 2 * TILE).astype(F32)
    bias_grad = bias_sum(extra[rows:]).reshape(-1)
    input_grad = jnp.sum(received[:, :TILE, :].astype(F32), axis=0).astype(BF16)
    return (hidden, input_grad, weight_grad, bias_grad)


def solution(mesh):
    src, dst = mesh.devices.shape
    fine = Mesh(mesh.devices.reshape(2, src // 4, 2, dst), ("ylo", "zq", "z0", "dst"))
    rows = P(("ylo", "zq", "z0", "dst"), None)
    placed = (
        rows,
        P(),
        P(),
        P(SRC, "dst", None),
        P(SRC, "dst", None),
        P(SRC, "dst", None, None),
        P(SRC, "dst", None, None),
        rows,
    )
    return jax.shard_map(
        body, mesh=fine, in_specs=placed, out_specs=(rows, rows, P(), P()), check_vma=False
    )
```

```python
import math

import jax
import jax.numpy as jnp
from jax import lax
from jax.experimental import pallas as pl
from jax.experimental.pallas import tpu as pltpu
from jax.sharding import Mesh, PartitionSpec as P

TILE = 128
BF16 = jnp.bfloat16
F32 = jnp.float32
NN = (((1,), (0,)), ((), ()))
NT = (((1,), (1,)), ((), ()))
TN = (((0,), (0,)), ((), ()))
SRC = ("ylo", "zq", "z0")
DST = ("x", "d0")
NEAR = ("ylo", "z0")
FAR = "zq"
GROUP = 32


def dot(a, b, dims=NN):
    return lax.dot_general(a, b, dims, preferred_element_type=F32)


def build_kernel(count_ref, pos_ref, weight_ref, tile_ref, pos_pairs, weight_pairs, *, backward):
    edges, slots = pos_ref.shape
    pairs = slots // 2
    positions = pos_ref[...].T
    weights = weight_ref[...].astype(F32).T
    pos_pairs[...] = jnp.concatenate([positions[:pairs], positions[pairs:]], axis=1)
    weight_pairs[...] = jnp.concatenate([weights[:pairs], weights[pairs:]], axis=1)
    lane = lax.broadcasted_iota(jnp.int32, (1, 2 * edges), 1)
    second = lane >= edges
    half = jnp.where(second, TILE, 0)
    one_rows = lax.broadcasted_iota(jnp.int32, (TILE, 2 * edges), 0)
    two_rows = lax.broadcasted_iota(jnp.int32, (2 * TILE, 2 * edges), 0)

    def one_pair(i, carry):
        limit = jnp.where(second, count_ref[i + pairs] + edges, count_ref[i])
        position = pos_pairs[pl.ds(i, 1), :]
        values = jnp.where(lane < limit, weight_pairs[pl.ds(i, 1), :], 0.0)
        row = position >> 7
        col = position & (TILE - 1)
        if backward:
            left = jnp.where(one_rows == col, 1.0, 0.0).astype(BF16)
            right = jnp.where(two_rows == row + half, values, 0.0).astype(BF16)
        else:
            left = jnp.where(one_rows == row, values, 0.0).astype(BF16)
            right = jnp.where(two_rows == col + half, 1.0, 0.0).astype(BF16)
        both = dot(left, right, NT).astype(BF16)
        tile_ref[i] = both[:, :TILE]
        tile_ref[i + pairs] = both[:, TILE:]
        return carry

    lax.fori_loop(0, pairs, one_pair, 0, unroll=4)


def spread_tiles(index_ref, tile_ref, rows_ref, sums, split, backward):
    shift = split.bit_length() - 1
    sums[...] = jnp.zeros_like(sums)

    def one_step(step, carry):
        found = []
        for i in range(GROUP):
            slot = step * GROUP + i
            index = index_ref[slot]
            target = index >> shift
            source = index & (split - 1)
            if backward:
                found.append((source, dot(tile_ref[slot], rows_ref[target])))
            else:
                found.append((target, dot(tile_ref[slot], rows_ref[source])))
        for place, value in found:
            sums[place] = sums[place] + value
        return carry

    lax.fori_loop(0, tile_ref.shape[0] // GROUP, one_step, 0)


def forward_kernel(index_ref, tile_ref, rows_ref, out_ref, sums):
    near, far = out_ref.shape[:2]
    spread_tiles(index_ref, tile_ref, rows_ref, sums, rows_ref.shape[0], False)
    for target in range(near * far):
        place = target // (2 * far) * 2 + target % 2
        out_ref[place, target // 2 % far] = sums[target].astype(BF16)


def high_low(value):
    high = value.astype(BF16).astype(F32)
    return high, value - high


def bias_tile(bias_rows):
    high, low = high_low(bias_rows[0:2])
    return jnp.concatenate([high, low, jnp.zeros((4, TILE), F32)], axis=0).astype(BF16)


def bias_sum(tile):
    return tile[0:2] + tile[2:4]


def dense_kernel(agg_ref, weight_ref, bias_ref, grad_ref, hidden_ref, send_ref, grad_pre_ref):
    aggregated = agg_ref[...]
    weight = weight_ref[...]
    preact = dot(aggregated, weight) + bias_ref[...]
    sigma = 1.0 / (1.0 + jnp.exp(-preact))
    hidden_ref[...] = (preact * sigma).astype(BF16)
    grad_pre = (grad_ref[...].astype(F32) * sigma * (1.0 + preact * (1.0 - sigma))).astype(BF16)
    grad_pre_ref[...] = grad_pre
    back_rows = dot(grad_pre, weight, NT).astype(BF16)
    send_ref[...] = jnp.broadcast_to(back_rows[None], send_ref.shape)


def part_kernel(agg_ref, grad_pre_ref, out_ref):
    grad_pre = grad_pre_ref[...]
    part = dot(agg_ref[...], grad_pre, TN)
    out_ref[:TILE] = part[:, :TILE]
    out_ref[TILE : 2 * TILE] = part[:, TILE:]
    bias_part = jnp.sum(grad_pre.astype(F32), axis=0, keepdims=True)
    bias_rows = [bias_part[:, :TILE], bias_part[:, TILE:], jnp.zeros((6, TILE), F32)]
    out_ref[2 * TILE :] = jnp.concatenate(bias_rows, axis=0)


def pick_kernel(place_ref, recv_ref, out_ref):
    peers = recv_ref.shape[0]
    size = out_ref.shape[0] - 8
    start = pl.multiple_of(place_ref[0] * size, 8)
    total = recv_ref[0, pl.ds(start, size), :]
    last = recv_ref[0, peers * size :, :]
    for k in range(1, peers):
        total = total + recv_ref[k, pl.ds(start, size), :]
        last = last + recv_ref[k, peers * size :, :]
    out_ref[:size] = total
    out_ref[size:] = last


def split_rows(total):
    high, low = high_low(total[:-8])
    return jnp.concatenate([high.astype(BF16), low.astype(BF16), bias_tile(total[-8:])], axis=0)


def join_rows(rows):
    count = (rows.shape[0] - 8) // 2
    bias_rows = jnp.concatenate([bias_sum(rows[2 * count :]), jnp.zeros((6, TILE), F32)], axis=0)
    return jnp.concatenate([rows[:count] + rows[count : 2 * count], bias_rows], axis=0)


def middle_kernel(place_ref, recv_ref, part_ref, out_ref):
    near = out_ref.shape[0]
    peers = part_ref.shape[0]
    top = recv_ref.shape[0] * TILE
    back_rows = recv_ref[...].reshape(top, TILE)
    size = (part_ref.shape[1] - 8) // peers
    start = pl.multiple_of(place_ref[0] * size, 8)
    total = part_ref[0, pl.ds(start, size), :]
    last = part_ref[0, peers * size :, :]
    for k in range(1, peers):
        total = total + part_ref[k, pl.ds(start, size), :]
        last = last + part_ref[k, peers * size :, :]
    extra = split_rows(jnp.concatenate([total, last], axis=0))
    for k in range(near):
        out_ref[k, :top] = back_rows
        out_ref[k, top:] = extra


def share_kernel(recv_ref, out_ref):
    top = recv_ref.shape[1] - out_ref.shape[1]
    total = jnp.sum(recv_ref[:, top:, :].astype(F32), axis=0)
    out_ref[...] = jnp.broadcast_to(split_rows(join_rows(total))[None], out_ref.shape)


def chunk_kernel(recv_ref, back_ref, out_ref, bias_grad_ref, *, scale):
    total = join_rows(jnp.sum(recv_ref[...].astype(F32), axis=0)) * scale
    size = total.shape[0] - 8
    bias_grad_ref[:, :TILE] = total[size : size + 1]
    bias_grad_ref[:, TILE:] = total[size + 1 : size + 2]
    high, low = high_low(total[:size])
    both = jnp.concatenate([high, low], axis=0).astype(BF16)
    out_ref[:, :TILE, :] = back_ref[...]
    out_ref[:, TILE:, :] = jnp.broadcast_to(both[None], (out_ref.shape[0], 2 * size, TILE))


def final_kernel(recv_ref, input_ref, weight_grad_ref, *, group):
    pieces = recv_ref.shape[0]
    input_ref[...] = jnp.sum(recv_ref[:, :TILE, :].astype(F32), axis=0).astype(BF16)
    size = 2 * TILE // pieces
    for d in range(pieces):
        start = ((d % group) * (pieces // group) + d // group) * size
        chunk = recv_ref[d, TILE : TILE + size, :].astype(F32) + recv_ref[d, TILE + size :, :].astype(F32)
        lane = start // TILE * TILE
        weight_grad_ref[start % TILE : start % TILE + size, lane : lane + TILE] = chunk


def backward_kernel(index_ref, tile_ref, recv_ref, out_ref, rows, sums):
    near = recv_ref.shape[0]
    far = rows.shape[0] // near
    pieces = out_ref.shape[0]
    for target in range(near * far):
        start = target // 2 % far * TILE
        rows[target] = recv_ref[target // (2 * far) * 2 + target % 2, start : start + TILE]
    spread_tiles(index_ref, tile_ref, rows, sums, pieces, True)
    out_ref[...] = sums[...].astype(BF16)


def vmem(n):
    return [pl.BlockSpec(memory_space=pltpu.VMEM)] * n


def smem(n):
    return [pl.BlockSpec(memory_space=pltpu.SMEM)] * n


def call(kernel, name, outs, scalars, arrays, scratch=(), **more):
    single = not isinstance(outs, tuple)
    return pl.pallas_call(
        kernel,
        out_shape=outs,
        in_specs=smem(len(scalars)) + vmem(len(arrays)),
        out_specs=vmem(1)[0] if single else tuple(vmem(len(outs))),
        scratch_shapes=list(scratch),
        compiler_params=pltpu.CompilerParams(vmem_limit_bytes=20 << 20),
        name=name,
        **more,
    )(*scalars, *arrays)


def shape(dims, dtype):
    return jax.ShapeDtypeStruct(dims, dtype)


def body(features, weight, bias, tile_index, edge_count, edge_pos, edge_weight, grad_out):
    near = lax.axis_size(NEAR)
    far = lax.axis_size(FAR)
    src = near * far
    dst = lax.axis_size(DST)
    index = tile_index.reshape(-1)
    counts = edge_count.reshape(-1)
    slots = counts.shape[0]
    positions = edge_pos.reshape(slots, -1).T
    weights = edge_weight.reshape(slots, -1).T
    edges = positions.shape[0]
    tile_shape = shape((slots, TILE, TILE), BF16)
    pair_scratch = (pltpu.VMEM((slots // 2, 2 * edges), jnp.int32), pltpu.VMEM((slots // 2, 2 * edges), F32))

    def build(positions, backward):
        return call(
            lambda *refs: build_kernel(*refs, backward=backward),
            "build_back" if backward else "build_tiles",
            tile_shape, (counts,), (positions, weights), pair_scratch,
        )

    sent = jnp.broadcast_to(features[None], (dst,) + features.shape)
    source_rows = lax.all_to_all(sent, DST, 0, 0, tiled=True)
    tiles = build(positions, False)
    partial = call(
        forward_kernel, "forward_tiles", shape((near, far, TILE, TILE), BF16),
        (index,), (tiles, source_rows), [pltpu.VMEM((src, TILE, TILE), F32)],
    )
    near_parts = lax.all_to_all(partial, NEAR, 0, 0, tiled=True)
    near_sums = jnp.sum(near_parts.astype(F32), axis=0).astype(BF16)
    late_positions, near_sums = lax.optimization_barrier((positions, near_sums))
    back_tiles = build(late_positions, True)
    parts = lax.all_to_all(near_sums, FAR, 0, 0, tiled=True)
    parts, back_tiles = lax.optimization_barrier((parts, back_tiles))
    aggregated = jnp.sum(parts.astype(F32), axis=0).astype(BF16)
    hidden, send, grad_pre = call(
        dense_kernel,
        "dense_layer",
        (shape(grad_out.shape, BF16), shape((far, TILE, TILE), BF16), shape(grad_out.shape, BF16)),
        (),
        (aggregated, weight, bias.reshape(1, -1), grad_out),
    )
    far_rows = lax.all_to_all(send, FAR, 0, 0, tiled=True)
    group = lax.axis_size("d0")
    part = call(part_kernel, "grad_part", shape((2 * TILE + 8, TILE), F32), (), (aggregated, grad_pre))
    part = lax.all_gather(part, "d0")
    part = call(
        pick_kernel, "grad_pick", shape((2 * TILE // group + 8, TILE), F32), (lax.axis_index("d0").reshape(1),), (part,)
    )
    part = lax.all_gather(part, "x")
    size = 2 * TILE // dst
    near_rows = call(
        middle_kernel, "middle_sums", shape((near, far * TILE + 2 * size + 8, TILE), BF16),
        (lax.axis_index("x").reshape(1),), (far_rows, part),
    )
    near_rows = lax.all_to_all(near_rows, NEAR, 0, 0, tiled=True)
    share = call(share_kernel, "grad_share", shape((far, 2 * size + 8, TILE), BF16), (), (near_rows,))
    shared = lax.all_to_all(share, FAR, 0, 0, tiled=True)
    back_send = call(
        backward_kernel, "backward_tiles", shape((dst, TILE, TILE), BF16),
        (index,), (back_tiles, near_rows),
        [pltpu.VMEM((src, TILE, TILE), BF16), pltpu.VMEM((dst, TILE, TILE), F32)],
    )
    node_scale = 1.0 / math.sqrt(features.shape[0] * src * dst)
    back_send, bias_grad = call(
        lambda *refs: chunk_kernel(*refs, scale=node_scale),
        "grad_chunk",
        (shape((dst, TILE + 2 * size, TILE), BF16), shape((1, 2 * TILE), F32)),
        (),
        (shared, back_send),
    )
    received = lax.all_to_all(back_send, DST, 0, 0, tiled=True)
    input_grad, weight_grad = call(
        lambda *refs: final_kernel(*refs, group=group),
        "final_sums",
        (shape(features.shape, BF16), shape((TILE, 2 * TILE), F32)),
        (),
        (received,),
    )
    return (hidden, input_grad, weight_grad, bias_grad.reshape(-1))


def solution(mesh):
    src, dst = mesh.devices.shape
    fine = Mesh(mesh.devices.reshape(2, src // 4, 2, dst // 4, 4), SRC + DST)
    rows = P(SRC + DST, None)
    placed = (
        rows,
        P(),
        P(),
        P(SRC, DST, None),
        P(SRC, DST, None),
        P(SRC, DST, None, None),
        P(SRC, DST, None, None),
        rows,
    )
    return jax.shard_map(
        body, mesh=fine, in_specs=placed, out_specs=(rows, rows, P(), P()), check_vma=False
    )
```

```python
import math

import jax
import jax.numpy as jnp
from jax import lax
from jax.experimental import pallas as pl
from jax.experimental.pallas import tpu as pltpu
from jax.sharding import Mesh, PartitionSpec as P

TILE = 128
BF16 = jnp.bfloat16
F32 = jnp.float32
NN = (((1,), (0,)), ((), ()))
NT = (((1,), (1,)), ((), ()))
TN = (((0,), (0,)), ((), ()))
SRC = ("ylo", "zq", "z0")
DST = ("x", "d0")
NEAR = ("ylo", "z0")
FAR = "zq"
GROUP = 32
CHUNKS = 4


def dot(a, b, dims=NN):
    return lax.dot_general(a, b, dims, preferred_element_type=F32)


def build_kernel(count_ref, pos_ref, weight_ref, tile_ref, pos_pairs, weight_pairs, *, backward):
    edges, slots = pos_ref.shape
    pairs = slots // 2
    positions = pos_ref[...].T
    weights = weight_ref[...].astype(F32).T
    pos_pairs[...] = jnp.concatenate([positions[:pairs], positions[pairs:]], axis=1)
    weight_pairs[...] = jnp.concatenate([weights[:pairs], weights[pairs:]], axis=1)
    lane = lax.broadcasted_iota(jnp.int32, (1, 2 * edges), 1)
    second = lane >= edges
    half = jnp.where(second, TILE, 0)
    one_rows = lax.broadcasted_iota(jnp.int32, (TILE, 2 * edges), 0)
    two_rows = lax.broadcasted_iota(jnp.int32, (2 * TILE, 2 * edges), 0)

    def one_pair(i, carry):
        limit = jnp.where(second, count_ref[i + pairs] + edges, count_ref[i])
        position = pos_pairs[pl.ds(i, 1), :]
        values = jnp.where(lane < limit, weight_pairs[pl.ds(i, 1), :], 0.0)
        row = position >> 7
        col = position & (TILE - 1)
        if backward:
            left = jnp.where(one_rows == col, 1.0, 0.0).astype(BF16)
            right = jnp.where(two_rows == row + half, values, 0.0).astype(BF16)
        else:
            left = jnp.where(one_rows == row, values, 0.0).astype(BF16)
            right = jnp.where(two_rows == col + half, 1.0, 0.0).astype(BF16)
        both = dot(left, right, NT).astype(BF16)
        tile_ref[i] = both[:, :TILE]
        tile_ref[i + pairs] = both[:, TILE:]
        return carry

    lax.fori_loop(0, pairs, one_pair, 0, unroll=4)


def spread_tiles(index_ref, tile_hbm, rows_ref, sums, tile_ref, sems, split, backward, ready):
    shift = split.bit_length() - 1
    slots = tile_ref.shape[0]
    chunk = slots // CHUNKS
    copies = []
    for c in range(CHUNKS):
        part = pl.ds(c * chunk, chunk)
        copies.append(pltpu.make_async_copy(tile_hbm.at[part], tile_ref.at[part], sems.at[c]))
    for copy in copies:
        copy.start()
    sums[...] = jnp.zeros_like(sums)
    ready()
    for start in range(0, slots, GROUP):
        if start % chunk == 0:
            copies[start // chunk].wait()
        found = []
        for slot in range(start, start + GROUP):
            index = index_ref[slot]
            target = index >> shift
            source = index & (split - 1)
            if backward:
                found.append((source, dot(tile_ref[slot], rows_ref[target])))
            else:
                found.append((target, dot(tile_ref[slot], rows_ref[source])))
        for place, value in found:
            sums[place] = sums[place] + value


def forward_kernel(index_ref, tile_hbm, rows_ref, out_ref, sums, tile_ref, sems):
    near, far = out_ref.shape[:2]
    split = rows_ref.shape[0]
    spread_tiles(index_ref, tile_hbm, rows_ref, sums, tile_ref, sems, split, False, lambda: None)
    for target in range(near * far):
        place = target // (2 * far) * 2 + target % 2
        out_ref[place, target // 2 % far] = sums[target].astype(BF16)


def high_low(value):
    high = value.astype(BF16).astype(F32)
    return high, value - high


def bias_tile(bias_rows):
    high, low = high_low(bias_rows[0:2])
    return jnp.concatenate([high, low, jnp.zeros((4, TILE), F32)], axis=0).astype(BF16)


def bias_sum(tile):
    return tile[0:2] + tile[2:4]


def dense_kernel(agg_ref, weight_ref, bias_ref, grad_ref, hidden_ref, send_ref, grad_pre_ref):
    aggregated = agg_ref[...]
    weight = weight_ref[...]
    preact = dot(aggregated, weight) + bias_ref[...]
    sigma = 1.0 / (1.0 + jnp.exp(-preact))
    hidden_ref[...] = (preact * sigma).astype(BF16)
    grad_pre = (grad_ref[...].astype(F32) * sigma * (1.0 + preact * (1.0 - sigma))).astype(BF16)
    grad_pre_ref[...] = grad_pre
    back_rows = dot(grad_pre, weight, NT).astype(BF16)
    send_ref[...] = jnp.broadcast_to(back_rows[None], send_ref.shape)


def part_kernel(agg_ref, grad_pre_ref, out_ref):
    grad_pre = grad_pre_ref[...]
    part = dot(agg_ref[...], grad_pre, TN)
    out_ref[:TILE] = part[:, :TILE]
    out_ref[TILE : 2 * TILE] = part[:, TILE:]
    bias_part = jnp.sum(grad_pre.astype(F32), axis=0, keepdims=True)
    bias_rows = [bias_part[:, :TILE], bias_part[:, TILE:], jnp.zeros((6, TILE), F32)]
    out_ref[2 * TILE :] = jnp.concatenate(bias_rows, axis=0)


def pick_kernel(place_ref, recv_ref, out_ref):
    peers = recv_ref.shape[0]
    size = out_ref.shape[0] - 8
    start = pl.multiple_of(place_ref[0] * size, 8)
    total = recv_ref[0, pl.ds(start, size), :]
    last = recv_ref[0, peers * size :, :]
    for k in range(1, peers):
        total = total + recv_ref[k, pl.ds(start, size), :]
        last = last + recv_ref[k, peers * size :, :]
    out_ref[:size] = total
    out_ref[size:] = last


def split_rows(total):
    high, low = high_low(total[:-8])
    return jnp.concatenate([high.astype(BF16), low.astype(BF16), bias_tile(total[-8:])], axis=0)


def join_rows(rows):
    count = (rows.shape[0] - 8) // 2
    bias_rows = jnp.concatenate([bias_sum(rows[2 * count :]), jnp.zeros((6, TILE), F32)], axis=0)
    return jnp.concatenate([rows[:count] + rows[count : 2 * count], bias_rows], axis=0)


def share_kernel(place_ref, part_ref, out_ref):
    peers = part_ref.shape[0]
    size = (part_ref.shape[1] - 8) // peers
    start = pl.multiple_of(place_ref[0] * size, 8)
    total = part_ref[0, pl.ds(start, size), :]
    last = part_ref[0, peers * size :, :]
    for k in range(1, peers):
        total = total + part_ref[k, pl.ds(start, size), :]
        last = last + part_ref[k, peers * size :, :]
    extra = split_rows(jnp.concatenate([total, last], axis=0))
    out_ref[...] = jnp.broadcast_to(extra[None], out_ref.shape)


def reshare_kernel(recv_ref, out_ref):
    total = jnp.sum(recv_ref[...].astype(F32), axis=0)
    out_ref[...] = jnp.broadcast_to(split_rows(join_rows(total))[None], out_ref.shape)


def chunk_kernel(recv_ref, back_ref, out_ref, bias_grad_ref, *, scale):
    total = join_rows(jnp.sum(recv_ref[...].astype(F32), axis=0)) * scale
    size = total.shape[0] - 8
    bias_grad_ref[:, :TILE] = total[size : size + 1]
    bias_grad_ref[:, TILE:] = total[size + 1 : size + 2]
    high, low = high_low(total[:size])
    both = jnp.concatenate([high, low], axis=0).astype(BF16)
    out_ref[:, :TILE, :] = back_ref[...]
    out_ref[:, TILE:, :] = jnp.broadcast_to(both[None], (out_ref.shape[0], 2 * size, TILE))


def final_kernel(recv_ref, input_ref, weight_grad_ref, *, group):
    pieces = recv_ref.shape[0]
    input_ref[...] = jnp.sum(recv_ref[:, :TILE, :].astype(F32), axis=0).astype(BF16)
    size = 2 * TILE // pieces
    for d in range(pieces):
        start = ((d % group) * (pieces // group) + d // group) * size
        chunk = recv_ref[d, TILE : TILE + size, :].astype(F32) + recv_ref[d, TILE + size :, :].astype(F32)
        lane = start // TILE * TILE
        weight_grad_ref[start % TILE : start % TILE + size, lane : lane + TILE] = chunk


def backward_kernel(index_ref, own_ref, tile_hbm, *rest):
    near_refs, (out_ref, sums, tile_ref, sems, rows) = rest[:-5], rest[-5:]
    far = near_refs[0].shape[0]
    pieces = out_ref.shape[0]

    def ready():
        for k, near_ref in enumerate(near_refs):
            other = own_ref[0] ^ k
            base = (other >> 1) * (2 * far) + (other & 1)
            for q in range(far):
                rows[base + 2 * q] = near_ref[q]

    spread_tiles(index_ref, tile_hbm, rows, sums, tile_ref, sems, pieces, True, ready)
    out_ref[...] = sums[...].astype(BF16)


def vmem(n):
    return [pl.BlockSpec(memory_space=pltpu.VMEM)] * n


def smem(n):
    return [pl.BlockSpec(memory_space=pltpu.SMEM)] * n


def call(kernel, name, outs, scalars, arrays, scratch=(), **more):
    single = not isinstance(outs, tuple)
    return pl.pallas_call(
        kernel,
        out_shape=outs,
        in_specs=smem(len(scalars)) + vmem(len(arrays)),
        out_specs=vmem(1)[0] if single else tuple(vmem(len(outs))),
        scratch_shapes=list(scratch),
        compiler_params=pltpu.CompilerParams(vmem_limit_bytes=20 << 20),
        name=name,
        **more,
    )(*scalars, *arrays)


def shape(dims, dtype):
    return jax.ShapeDtypeStruct(dims, dtype)


def spread(kernel, name, out, scalars, tiles, arrays, scratch):
    return pl.pallas_call(
        kernel,
        out_shape=out,
        in_specs=smem(len(scalars)) + [pl.BlockSpec(memory_space=pltpu.HBM)] + vmem(len(arrays)),
        out_specs=vmem(1)[0],
        scratch_shapes=scratch,
        compiler_params=pltpu.CompilerParams(vmem_limit_bytes=20 << 20),
        name=name,
    )(*scalars, pltpu.with_memory_space_constraint(tiles, pltpu.HBM), *arrays)


def swap(array, step, axis):
    return lax.ppermute(array, axis, [(i, i ^ step) for i in range(lax.axis_size(axis))])


def body(features, weight, bias, tile_index, edge_count, edge_pos, edge_weight, grad_out):
    near = lax.axis_size(NEAR)
    far = lax.axis_size(FAR)
    src = near * far
    dst = lax.axis_size(DST)
    index = tile_index.reshape(-1)
    counts = edge_count.reshape(-1)
    slots = counts.shape[0]
    positions = edge_pos.reshape(slots, -1).T
    weights = edge_weight.reshape(slots, -1).T
    edges = positions.shape[0]
    tile_shape = pltpu.HBM((slots, TILE, TILE), BF16)
    pair_scratch = (pltpu.VMEM((slots // 2, 2 * edges), jnp.int32), pltpu.VMEM((slots // 2, 2 * edges), F32))

    def build(positions, backward):
        return call(
            lambda *refs: build_kernel(*refs, backward=backward),
            "build_back" if backward else "build_tiles",
            tile_shape, (counts,), (positions, weights), pair_scratch,
        )

    sent = jnp.broadcast_to(features[None], (dst,) + features.shape)
    source_rows = lax.all_to_all(sent, DST, 0, 0, tiled=True)
    tiles = build(positions, False)
    tile_scratch = [pltpu.VMEM((slots, TILE, TILE), BF16), pltpu.SemaphoreType.DMA((CHUNKS,))]
    partial = spread(
        forward_kernel, "forward_tiles", shape((near, far, TILE, TILE), BF16),
        (index,), tiles, (source_rows,), [pltpu.VMEM((src, TILE, TILE), F32)] + tile_scratch,
    )
    near_parts = lax.all_to_all(partial, NEAR, 0, 0, tiled=True)
    near_sums = jnp.sum(near_parts.astype(F32), axis=0).astype(BF16)
    late_positions, near_sums = lax.optimization_barrier((positions, near_sums))
    back_tiles = build(late_positions, True)
    parts = lax.all_to_all(near_sums, FAR, 0, 0, tiled=True)
    parts, back_tiles = lax.optimization_barrier((parts, back_tiles))
    aggregated = jnp.sum(parts.astype(F32), axis=0).astype(BF16)
    hidden, send, grad_pre = call(
        dense_kernel,
        "dense_layer",
        (shape(grad_out.shape, BF16), shape((far, TILE, TILE), BF16), shape(grad_out.shape, BF16)),
        (),
        (aggregated, weight, bias.reshape(1, -1), grad_out),
    )
    far_rows = lax.all_to_all(send, FAR, 0, 0, tiled=True)
    group = lax.axis_size("d0")
    part = call(part_kernel, "grad_part", shape((2 * TILE + 8, TILE), F32), (), (aggregated, grad_pre))
    part = lax.all_gather(part, "d0")
    part = call(
        pick_kernel, "grad_pick", shape((2 * TILE // group + 8, TILE), F32), (lax.axis_index("d0").reshape(1),), (part,)
    )
    part = lax.all_gather(part, "x")
    size = 2 * TILE // dst
    share = call(
        share_kernel, "grad_share", shape((far, 2 * size + 8, TILE), BF16), (lax.axis_index("x").reshape(1),), (part,)
    )
    shared = lax.all_to_all(share, FAR, 0, 0, tiled=True)
    near_all = [far_rows] + [swap(far_rows, k, NEAR) for k in range(1, near)]
    share = call(reshare_kernel, "grad_reshare", shape((near, 2 * size + 8, TILE), BF16), (), (shared,))
    shared = lax.all_to_all(share, NEAR, 0, 0, tiled=True)
    back_send = spread(
        backward_kernel, "backward_tiles", shape((dst, TILE, TILE), BF16),
        (index, lax.axis_index(NEAR).reshape(1)), back_tiles, near_all,
        [pltpu.VMEM((dst, TILE, TILE), F32)] + tile_scratch + [pltpu.VMEM((src, TILE, TILE), BF16)],
    )
    node_scale = 1.0 / math.sqrt(features.shape[0] * src * dst)
    back_send, bias_grad = call(
        lambda *refs: chunk_kernel(*refs, scale=node_scale),
        "grad_chunk",
        (shape((dst, TILE + 2 * size, TILE), BF16), shape((1, 2 * TILE), F32)),
        (),
        (shared, back_send),
    )
    received = lax.all_to_all(back_send, DST, 0, 0, tiled=True)
    input_grad, weight_grad = call(
        lambda *refs: final_kernel(*refs, group=group),
        "final_sums",
        (shape(features.shape, BF16), shape((TILE, 2 * TILE), F32)),
        (),
        (received,),
    )
    return (hidden, input_grad, weight_grad, bias_grad.reshape(-1))


def solution(mesh):
    src, dst = mesh.devices.shape
    fine = Mesh(mesh.devices.reshape(2, src // 4, 2, dst // 4, 4), SRC + DST)
    rows = P(SRC + DST, None)
    placed = (
        rows,
        P(),
        P(),
        P(SRC, DST, None),
        P(SRC, DST, None),
        P(SRC, DST, None, None),
        P(SRC, DST, None, None),
        rows,
    )
    return jax.shard_map(
        body, mesh=fine, in_specs=placed, out_specs=(rows, rows, P(), P()), check_vma=False
    )
```

```python
import math

import jax
import jax.numpy as jnp
from jax import lax
from jax.experimental import pallas as pl
from jax.experimental.pallas import tpu as pltpu
from jax.sharding import Mesh, PartitionSpec as P

TILE = 128
BF16 = jnp.bfloat16
F32 = jnp.float32
NN = (((1,), (0,)), ((), ()))
NT = (((1,), (1,)), ((), ()))
TN = (((0,), (0,)), ((), ()))
SRC = ("ylo", "zq", "z0")
DST = ("x", "d0")
NEAR = ("ylo", "z0")
FAR = "zq"
GROUP = 32
CHUNKS = 4


def dot(a, b, dims=NN):
    return lax.dot_general(a, b, dims, preferred_element_type=F32)


def build_kernel(count_ref, pos_ref, weight_ref, tile_ref, pos_pairs, weight_pairs, *, backward):
    edges, slots = pos_ref.shape
    pairs = slots // 2
    positions = pos_ref[...].T
    weights = weight_ref[...].astype(F32).T
    pos_pairs[...] = jnp.concatenate([positions[:pairs], positions[pairs:]], axis=1)
    weight_pairs[...] = jnp.concatenate([weights[:pairs], weights[pairs:]], axis=1)
    lane = lax.broadcasted_iota(jnp.int32, (1, 2 * edges), 1)
    second = lane >= edges
    half = jnp.where(second, TILE, 0)
    one_rows = lax.broadcasted_iota(jnp.int32, (TILE, 2 * edges), 0)
    two_rows = lax.broadcasted_iota(jnp.int32, (2 * TILE, 2 * edges), 0)

    def one_pair(i, carry):
        limit = jnp.where(second, count_ref[i + pairs] + edges, count_ref[i])
        position = pos_pairs[pl.ds(i, 1), :]
        values = jnp.where(lane < limit, weight_pairs[pl.ds(i, 1), :], 0.0)
        row = position >> 7
        col = position & (TILE - 1)
        if backward:
            left = jnp.where(one_rows == col, 1.0, 0.0).astype(BF16)
            right = jnp.where(two_rows == row + half, values, 0.0).astype(BF16)
        else:
            left = jnp.where(one_rows == row, values, 0.0).astype(BF16)
            right = jnp.where(two_rows == col + half, 1.0, 0.0).astype(BF16)
        both = dot(left, right, NT).astype(BF16)
        tile_ref[i] = both[:, :TILE]
        tile_ref[i + pairs] = both[:, TILE:]
        return carry

    lax.fori_loop(0, pairs, one_pair, 0, unroll=4)


def spread_tiles(index_ref, tile_hbm, rows_ref, sums, tile_ref, sems, split, backward, ready):
    shift = split.bit_length() - 1
    slots = tile_ref.shape[0]
    chunk = slots // CHUNKS
    copies = []
    for c in range(CHUNKS):
        part = pl.ds(c * chunk, chunk)
        copies.append(pltpu.make_async_copy(tile_hbm.at[part], tile_ref.at[part], sems.at[c]))
    for copy in copies:
        copy.start()
    sums[...] = jnp.zeros_like(sums)
    ready()
    for start in range(0, slots, GROUP):
        if start % chunk == 0:
            copies[start // chunk].wait()
        found = []
        for slot in range(start, start + GROUP):
            index = index_ref[slot]
            target = index >> shift
            source = index & (split - 1)
            if backward:
                found.append((source, dot(tile_ref[slot], rows_ref[target])))
            else:
                found.append((target, dot(tile_ref[slot], rows_ref[source])))
        for place, value in found:
            sums[place] = sums[place] + value


def forward_kernel(index_ref, tile_hbm, rows_ref, out_ref, sums, tile_ref, sems):
    near, far = out_ref.shape[:2]
    split = rows_ref.shape[0]
    spread_tiles(index_ref, tile_hbm, rows_ref, sums, tile_ref, sems, split, False, lambda: None)
    for target in range(near * far):
        place = target // (2 * far) * 2 + target % 2
        out_ref[place, target // 2 % far] = sums[target].astype(BF16)


def high_low(value):
    high = value.astype(BF16).astype(F32)
    return high, value - high


def bias_tile(bias_rows):
    high, low = high_low(bias_rows[0:2])
    return jnp.concatenate([high, low, jnp.zeros((4, TILE), F32)], axis=0).astype(BF16)


def bias_sum(tile):
    return tile[0:2] + tile[2:4]


def dense_kernel(agg_ref, weight_ref, bias_ref, grad_ref, hidden_ref, send_ref, grad_pre_ref):
    aggregated = agg_ref[...]
    weight = weight_ref[...]
    preact = dot(aggregated, weight) + bias_ref[...]
    sigma = 1.0 / (1.0 + jnp.exp(-preact))
    hidden_ref[...] = (preact * sigma).astype(BF16)
    grad_pre = (grad_ref[...].astype(F32) * sigma * (1.0 + preact * (1.0 - sigma))).astype(BF16)
    grad_pre_ref[...] = grad_pre
    back_rows = dot(grad_pre, weight, NT).astype(BF16)
    send_ref[...] = jnp.broadcast_to(back_rows[None], send_ref.shape)


def part_kernel(agg_ref, grad_pre_ref, out_ref):
    grad_pre = grad_pre_ref[...]
    part = dot(agg_ref[...], grad_pre, TN).astype(BF16)
    out_ref[:TILE] = part[:, :TILE]
    out_ref[TILE : 2 * TILE] = part[:, TILE:]
    bias_part = jnp.sum(grad_pre.astype(F32), axis=0, keepdims=True)
    out_ref[2 * TILE :] = bias_tile(jnp.concatenate([bias_part[:, :TILE], bias_part[:, TILE:]], axis=0))


def pick_rows(place, recv_ref, size):
    peers = recv_ref.shape[0]
    start = pl.multiple_of(place * size, 8)
    total = recv_ref[0, pl.ds(start, size), :].astype(F32)
    last = recv_ref[0, peers * size :, :].astype(F32)
    for k in range(1, peers):
        total = total + recv_ref[k, pl.ds(start, size), :].astype(F32)
        last = last + recv_ref[k, peers * size :, :].astype(F32)
    return total, last


def pick_kernel(place_ref, recv_ref, out_ref):
    size = out_ref.shape[0] - 8
    out_ref[:size], out_ref[size:] = pick_rows(place_ref[0], recv_ref, size)


def share_kernel(place_ref, part_ref, out_ref):
    size = (part_ref.shape[1] - 8) // part_ref.shape[0]
    total, last = pick_rows(place_ref[0], part_ref, size)
    rows = jnp.concatenate([total.astype(BF16), bias_tile(bias_sum(last))], axis=0)
    out_ref[...] = jnp.broadcast_to(rows[None], out_ref.shape)


def reshare_kernel(recv_ref, out_ref):
    total = jnp.sum(recv_ref[...].astype(F32), axis=0)
    size = (out_ref.shape[1] - 8) // 2
    high, low = high_low(total[:size])
    rows = [high.astype(BF16), low.astype(BF16), bias_tile(bias_sum(total[size:]))]
    out_ref[...] = jnp.broadcast_to(jnp.concatenate(rows, axis=0)[None], out_ref.shape)


def chunk_kernel(recv_ref, back_ref, out_ref, bias_grad_ref, *, scale):
    total = jnp.sum(recv_ref[...].astype(F32), axis=0) * scale
    size = (total.shape[0] - 8) // 2
    bias_rows = bias_sum(total[2 * size :])
    bias_grad_ref[:, :TILE] = bias_rows[0:1]
    bias_grad_ref[:, TILE:] = bias_rows[1:2]
    chunk = (total[:size] + total[size : 2 * size]).astype(BF16)
    out_ref[:, :TILE, :] = back_ref[...]
    out_ref[:, TILE:, :] = jnp.broadcast_to(chunk[None], (out_ref.shape[0], size, TILE))


def copies_kernel(rows_ref, out_ref):
    out_ref[...] = jnp.broadcast_to(rows_ref[...][None], out_ref.shape)


def final_kernel(recv_ref, input_ref, weight_grad_ref, *, group):
    pieces = recv_ref.shape[0]
    input_ref[...] = jnp.sum(recv_ref[:, :TILE, :].astype(F32), axis=0).astype(BF16)
    size = 2 * TILE // pieces
    for d in range(pieces):
        start = ((d % group) * (pieces // group) + d // group) * size
        chunk = recv_ref[d, TILE:, :].astype(F32)
        lane = start // TILE * TILE
        weight_grad_ref[start % TILE : start % TILE + size, lane : lane + TILE] = chunk


def backward_kernel(index_ref, own_ref, tile_hbm, *rest):
    near_refs, (out_ref, sums, tile_ref, sems, rows) = rest[:-5], rest[-5:]
    far = near_refs[0].shape[0]
    pieces = out_ref.shape[0]

    def ready():
        for k, near_ref in enumerate(near_refs):
            other = own_ref[0] ^ k
            base = (other >> 1) * (2 * far) + (other & 1)
            for q in range(far):
                rows[base + 2 * q] = near_ref[q]

    spread_tiles(index_ref, tile_hbm, rows, sums, tile_ref, sems, pieces, True, ready)
    out_ref[...] = sums[...].astype(BF16)


def vmem(n):
    return [pl.BlockSpec(memory_space=pltpu.VMEM)] * n


def smem(n):
    return [pl.BlockSpec(memory_space=pltpu.SMEM)] * n


def call(kernel, name, outs, scalars, arrays, scratch=(), **more):
    single = not isinstance(outs, tuple)
    return pl.pallas_call(
        kernel,
        out_shape=outs,
        in_specs=smem(len(scalars)) + vmem(len(arrays)),
        out_specs=vmem(1)[0] if single else tuple(vmem(len(outs))),
        scratch_shapes=list(scratch),
        compiler_params=pltpu.CompilerParams(vmem_limit_bytes=20 << 20),
        name=name,
        **more,
    )(*scalars, *arrays)


def shape(dims, dtype):
    return jax.ShapeDtypeStruct(dims, dtype)


def spread(kernel, name, out, scalars, tiles, arrays, scratch):
    return pl.pallas_call(
        kernel,
        out_shape=out,
        in_specs=smem(len(scalars)) + [pl.BlockSpec(memory_space=pltpu.HBM)] + vmem(len(arrays)),
        out_specs=vmem(1)[0],
        scratch_shapes=scratch,
        compiler_params=pltpu.CompilerParams(vmem_limit_bytes=20 << 20),
        name=name,
    )(*scalars, pltpu.with_memory_space_constraint(tiles, pltpu.HBM), *arrays)


def swap(array, step, axis):
    return lax.ppermute(array, axis, [(i, i ^ step) for i in range(lax.axis_size(axis))])


def body(features, weight, bias, tile_index, edge_count, edge_pos, edge_weight, grad_out):
    near = lax.axis_size(NEAR)
    far = lax.axis_size(FAR)
    src = near * far
    dst = lax.axis_size(DST)
    index = tile_index.reshape(-1)
    counts = edge_count.reshape(-1)
    slots = counts.shape[0]
    positions = edge_pos.reshape(slots, -1).T
    weights = edge_weight.reshape(slots, -1).T
    edges = positions.shape[0]
    tile_shape = pltpu.HBM((slots, TILE, TILE), BF16)
    pair_scratch = (pltpu.VMEM((slots // 2, 2 * edges), jnp.int32), pltpu.VMEM((slots // 2, 2 * edges), F32))

    def build(positions, backward):
        return call(
            lambda *refs: build_kernel(*refs, backward=backward),
            "build_back" if backward else "build_tiles",
            tile_shape, (counts,), (positions, weights), pair_scratch,
        )

    sent = call(copies_kernel, "feature_copies", shape((dst,) + features.shape, BF16), (), (features,))
    source_rows = lax.all_to_all(sent, DST, 0, 0, tiled=True)
    tiles = build(positions, False)
    tile_scratch = [pltpu.VMEM((slots, TILE, TILE), BF16), pltpu.SemaphoreType.DMA((CHUNKS,))]
    partial = spread(
        forward_kernel, "forward_tiles", shape((near, far, TILE, TILE), BF16),
        (index,), tiles, (source_rows,), [pltpu.VMEM((src, TILE, TILE), F32)] + tile_scratch,
    )
    near_parts = lax.all_to_all(partial, NEAR, 0, 0, tiled=True)
    near_sums = jnp.sum(near_parts.astype(F32), axis=0).astype(BF16)
    late_positions, near_sums = lax.optimization_barrier((positions, near_sums))
    back_tiles = build(late_positions, True)
    parts = lax.all_to_all(near_sums, FAR, 0, 0, tiled=True)
    parts, back_tiles = lax.optimization_barrier((parts, back_tiles))
    aggregated = jnp.sum(parts.astype(F32), axis=0).astype(BF16)
    hidden, send, grad_pre = call(
        dense_kernel,
        "dense_layer",
        (shape(grad_out.shape, BF16), shape((far, TILE, TILE), BF16), shape(grad_out.shape, BF16)),
        (),
        (aggregated, weight, bias.reshape(1, -1), grad_out),
    )
    far_rows = lax.all_to_all(send, FAR, 0, 0, tiled=True)
    group = lax.axis_size("d0")
    part = call(part_kernel, "grad_part", shape((2 * TILE + 8, TILE), BF16), (), (aggregated, grad_pre))
    part = lax.all_gather(part, "d0")
    part = call(
        pick_kernel, "grad_pick", shape((2 * TILE // group + 8, TILE), F32), (lax.axis_index("d0").reshape(1),), (part,)
    )
    part = lax.all_gather(part, "x")
    size = 2 * TILE // dst
    share = call(
        share_kernel, "grad_share", shape((far, size + 8, TILE), BF16), (lax.axis_index("x").reshape(1),), (part,)
    )
    shared = lax.all_to_all(share, FAR, 0, 0, tiled=True)
    near_all = [far_rows] + [swap(far_rows, k, NEAR) for k in range(1, near)]
    share = call(reshare_kernel, "grad_reshare", shape((near, 2 * size + 8, TILE), BF16), (), (shared,))
    shared = lax.all_to_all(share, NEAR, 0, 0, tiled=True)
    back_send = spread(
        backward_kernel, "backward_tiles", shape((dst, TILE, TILE), BF16),
        (index, lax.axis_index(NEAR).reshape(1)), back_tiles, near_all,
        [pltpu.VMEM((dst, TILE, TILE), F32)] + tile_scratch + [pltpu.VMEM((src, TILE, TILE), BF16)],
    )
    node_scale = 1.0 / math.sqrt(features.shape[0] * src * dst)
    back_send, bias_grad = call(
        lambda *refs: chunk_kernel(*refs, scale=node_scale),
        "grad_chunk",
        (shape((dst, TILE + size, TILE), BF16), shape((1, 2 * TILE), F32)),
        (),
        (shared, back_send),
    )
    received = lax.all_to_all(back_send, DST, 0, 0, tiled=True)
    input_grad, weight_grad = call(
        lambda *refs: final_kernel(*refs, group=group),
        "final_sums",
        (shape(features.shape, BF16), shape((TILE, 2 * TILE), F32)),
        (),
        (received,),
    )
    return (hidden, input_grad, weight_grad, bias_grad.reshape(-1))


def solution(mesh):
    src, dst = mesh.devices.shape
    fine = Mesh(mesh.devices.reshape(2, src // 4, 2, dst // 4, 4), SRC + DST)
    rows = P(SRC + DST, None)
    placed = (
        rows,
        P(),
        P(),
        P(SRC, DST, None),
        P(SRC, DST, None),
        P(SRC, DST, None, None),
        P(SRC, DST, None, None),
        rows,
    )
    return jax.shard_map(
        body, mesh=fine, in_specs=placed, out_specs=(rows, rows, P(), P()), check_vma=False
    )
```

```python
import math

import jax
import jax.numpy as jnp
from jax import lax
from jax.experimental import pallas as pl
from jax.experimental.pallas import tpu as pltpu
from jax.sharding import Mesh, PartitionSpec as P

TILE = 128
BF16 = jnp.bfloat16
F32 = jnp.float32
NN = (((1,), (0,)), ((), ()))
NT = (((1,), (1,)), ((), ()))
TN = (((0,), (0,)), ((), ()))
SRC = ("ylo", "zq", "z0")
DST = ("x1", "x0", "d0")
NEAR = ("ylo", "z0")
FAR = "zq"
GROUP = 32
CHUNKS = 4


def dot(a, b, dims=NN):
    return lax.dot_general(a, b, dims, preferred_element_type=F32)


def build_kernel(count_ref, pos_ref, weight_ref, tile_ref, pos_pairs, weight_pairs, *, backward):
    edges, slots = pos_ref.shape
    pairs = slots // 2
    positions = pos_ref[...].T
    weights = weight_ref[...].astype(F32).T
    pos_pairs[...] = jnp.concatenate([positions[:pairs], positions[pairs:]], axis=1)
    weight_pairs[...] = jnp.concatenate([weights[:pairs], weights[pairs:]], axis=1)
    lane = lax.broadcasted_iota(jnp.int32, (1, 2 * edges), 1)
    second = lane >= edges
    half = jnp.where(second, TILE, 0)
    one_rows = lax.broadcasted_iota(jnp.int32, (TILE, 2 * edges), 0)
    two_rows = lax.broadcasted_iota(jnp.int32, (2 * TILE, 2 * edges), 0)

    def one_pair(i, carry):
        limit = jnp.where(second, count_ref[i + pairs] + edges, count_ref[i])
        position = pos_pairs[pl.ds(i, 1), :]
        values = jnp.where(lane < limit, weight_pairs[pl.ds(i, 1), :], 0.0)
        row = position >> 7
        col = position & (TILE - 1)
        if backward:
            left = jnp.where(one_rows == col, 1.0, 0.0).astype(BF16)
            right = jnp.where(two_rows == row + half, values, 0.0).astype(BF16)
        else:
            left = jnp.where(one_rows == row, values, 0.0).astype(BF16)
            right = jnp.where(two_rows == col + half, 1.0, 0.0).astype(BF16)
        both = dot(left, right, NT).astype(BF16)
        tile_ref[i] = both[:, :TILE]
        tile_ref[i + pairs] = both[:, TILE:]
        return carry

    lax.fori_loop(0, pairs, one_pair, 0, unroll=4)


def spread_tiles(index_ref, tile_hbm, rows_ref, sums, tile_ref, sems, split, backward, ready):
    shift = split.bit_length() - 1
    slots = tile_ref.shape[0]
    chunk = slots // CHUNKS
    copies = []
    for c in range(CHUNKS):
        part = pl.ds(c * chunk, chunk)
        copies.append(pltpu.make_async_copy(tile_hbm.at[part], tile_ref.at[part], sems.at[c]))
    for copy in copies:
        copy.start()
    sums[...] = jnp.zeros_like(sums)
    ready()
    for start in range(0, slots, GROUP):
        if start % chunk == 0:
            copies[start // chunk].wait()
        found = []
        for slot in range(start, start + GROUP):
            index = index_ref[slot]
            target = index >> shift
            source = index & (split - 1)
            if backward:
                found.append((source, dot(tile_ref[slot], rows_ref[target])))
            else:
                found.append((target, dot(tile_ref[slot], rows_ref[source])))
        for place, value in found:
            sums[place] = sums[place] + value


def forward_kernel(index_ref, tile_hbm, rows_ref, out_ref, sums, tile_ref, sems):
    near, far = out_ref.shape[:2]
    split = rows_ref.shape[0]
    spread_tiles(index_ref, tile_hbm, rows_ref, sums, tile_ref, sems, split, False, lambda: None)
    for target in range(near * far):
        place = target // (2 * far) * 2 + target % 2
        out_ref[place, target // 2 % far] = sums[target].astype(BF16)


def high_low(value):
    high = value.astype(BF16).astype(F32)
    return high, value - high


def bias_tile(bias_rows):
    high, low = high_low(bias_rows[0:2])
    return jnp.concatenate([high, low, jnp.zeros((4, TILE), F32)], axis=0).astype(BF16)


def bias_sum(tile):
    return tile[0:2] + tile[2:4]


def dense_kernel(agg_ref, weight_ref, bias_ref, grad_ref, hidden_ref, send_ref, grad_pre_ref):
    aggregated = agg_ref[...]
    weight = weight_ref[...]
    preact = dot(aggregated, weight) + bias_ref[...]
    sigma = 1.0 / (1.0 + jnp.exp(-preact))
    hidden_ref[...] = (preact * sigma).astype(BF16)
    grad_pre = (grad_ref[...].astype(F32) * sigma * (1.0 + preact * (1.0 - sigma))).astype(BF16)
    grad_pre_ref[...] = grad_pre
    back_rows = dot(grad_pre, weight, NT).astype(BF16)
    send_ref[...] = jnp.broadcast_to(back_rows[None], send_ref.shape)


def part_kernel(agg_ref, grad_pre_ref, out_ref):
    grad_pre = grad_pre_ref[...]
    part = dot(agg_ref[...], grad_pre, TN).astype(BF16)
    out_ref[:TILE] = part[:, :TILE]
    out_ref[TILE : 2 * TILE] = part[:, TILE:]
    bias_part = jnp.sum(grad_pre.astype(F32), axis=0, keepdims=True)
    out_ref[2 * TILE :] = bias_tile(jnp.concatenate([bias_part[:, :TILE], bias_part[:, TILE:]], axis=0))


def pick_rows(place, recv_ref, size):
    peers = recv_ref.shape[0]
    start = pl.multiple_of(place * size, 8)
    total = recv_ref[0, pl.ds(start, size), :].astype(F32)
    last = recv_ref[0, peers * size :, :].astype(F32)
    for k in range(1, peers):
        total = total + recv_ref[k, pl.ds(start, size), :].astype(F32)
        last = last + recv_ref[k, peers * size :, :].astype(F32)
    return total, last


def pick_kernel(place_ref, recv_ref, out_ref):
    size = out_ref.shape[0] - 8
    out_ref[:size], out_ref[size:] = pick_rows(place_ref[0], recv_ref, size)


def share_kernel(place_ref, part_ref, out_ref):
    size = (part_ref.shape[1] - 8) // part_ref.shape[0]
    total, last = pick_rows(place_ref[0], part_ref, size)
    rows = jnp.concatenate([total.astype(BF16), bias_tile(bias_sum(last))], axis=0)
    out_ref[...] = jnp.broadcast_to(rows[None], out_ref.shape)


def reshare_kernel(recv_ref, out_ref):
    total = jnp.sum(recv_ref[...].astype(F32), axis=0)
    size = (out_ref.shape[1] - 8) // 2
    high, low = high_low(total[:size])
    rows = [high.astype(BF16), low.astype(BF16), bias_tile(bias_sum(total[size:]))]
    out_ref[...] = jnp.broadcast_to(jnp.concatenate(rows, axis=0)[None], out_ref.shape)


def chunk_kernel(recv_ref, back_ref, out_ref, bias_grad_ref, *, scale):
    total = jnp.sum(recv_ref[...].astype(F32), axis=0) * scale
    size = (total.shape[0] - 8) // 2
    bias_rows = bias_sum(total[2 * size :])
    bias_grad_ref[:, :TILE] = bias_rows[0:1]
    bias_grad_ref[:, TILE:] = bias_rows[1:2]
    chunk = (total[:size] + total[size : 2 * size]).astype(BF16)
    out_ref[:, :TILE, :] = back_ref[...]
    out_ref[:, TILE:, :] = jnp.broadcast_to(chunk[None], (out_ref.shape[0], size, TILE))


def copies_kernel(rows_hbm, out_ref, rows_ref, sem):
    copy = pltpu.make_async_copy(rows_hbm, rows_ref, sem)
    copy.start()
    copy.wait()
    out_ref[...] = jnp.broadcast_to(rows_ref[...][None], out_ref.shape)


def final_kernel(recv_ref, input_ref, weight_grad_ref, *, group):
    pieces = recv_ref.shape[0]
    input_ref[...] = jnp.sum(recv_ref[:, :TILE, :].astype(F32), axis=0).astype(BF16)
    size = 2 * TILE // pieces
    for d in range(pieces):
        start = ((d % group) * (pieces // group) + d // group) * size
        chunk = recv_ref[d, TILE:, :].astype(F32)
        lane = start // TILE * TILE
        weight_grad_ref[start % TILE : start % TILE + size, lane : lane + TILE] = chunk


def backward_kernel(index_ref, own_ref, tile_hbm, *rest):
    near_refs, (out_ref, sums, tile_ref, sems, rows) = rest[:-5], rest[-5:]
    far = near_refs[0].shape[0]
    pieces = out_ref.shape[0]

    def ready():
        for k, near_ref in enumerate(near_refs):
            other = own_ref[0] ^ k
            base = (other >> 1) * (2 * far) + (other & 1)
            for q in range(far):
                rows[base + 2 * q] = near_ref[q]

    spread_tiles(index_ref, tile_hbm, rows, sums, tile_ref, sems, pieces, True, ready)
    out_ref[...] = sums[...].astype(BF16)


def vmem(n):
    return [pl.BlockSpec(memory_space=pltpu.VMEM)] * n


def smem(n):
    return [pl.BlockSpec(memory_space=pltpu.SMEM)] * n


def call(kernel, name, outs, scalars, arrays, scratch=(), **more):
    single = not isinstance(outs, tuple)
    return pl.pallas_call(
        kernel,
        out_shape=outs,
        in_specs=smem(len(scalars)) + vmem(len(arrays)),
        out_specs=vmem(1)[0] if single else tuple(vmem(len(outs))),
        scratch_shapes=list(scratch),
        compiler_params=pltpu.CompilerParams(vmem_limit_bytes=20 << 20),
        name=name,
        **more,
    )(*scalars, *arrays)


def shape(dims, dtype):
    return jax.ShapeDtypeStruct(dims, dtype)


def spread(kernel, name, out, scalars, tiles, arrays, scratch):
    return pl.pallas_call(
        kernel,
        out_shape=out,
        in_specs=smem(len(scalars)) + [pl.BlockSpec(memory_space=pltpu.HBM)] + vmem(len(arrays)),
        out_specs=vmem(1)[0],
        scratch_shapes=scratch,
        compiler_params=pltpu.CompilerParams(vmem_limit_bytes=20 << 20),
        name=name,
    )(*scalars, pltpu.with_memory_space_constraint(tiles, pltpu.HBM), *arrays)


def swap(array, step, axis):
    return lax.ppermute(array, axis, [(i, i ^ step) for i in range(lax.axis_size(axis))])


def body(features, weight, bias, tile_index, edge_count, edge_pos, edge_weight, grad_out):
    near = lax.axis_size(NEAR)
    far = lax.axis_size(FAR)
    src = near * far
    dst = lax.axis_size(DST)
    index = tile_index.reshape(-1)
    counts = edge_count.reshape(-1)
    slots = counts.shape[0]
    positions = edge_pos.reshape(slots, -1).T
    weights = edge_weight.reshape(slots, -1).T
    edges = positions.shape[0]
    tile_shape = pltpu.HBM((slots, TILE, TILE), BF16)
    pair_scratch = (pltpu.VMEM((slots // 2, 2 * edges), jnp.int32), pltpu.VMEM((slots // 2, 2 * edges), F32))

    def build(positions, backward):
        return call(
            lambda *refs: build_kernel(*refs, backward=backward),
            "build_back" if backward else "build_tiles",
            tile_shape, (counts,), (positions, weights), pair_scratch,
        )

    sent = pl.pallas_call(
        copies_kernel,
        out_shape=shape((dst,) + features.shape, BF16),
        in_specs=[pl.BlockSpec(memory_space=pltpu.HBM)],
        out_specs=vmem(1)[0],
        scratch_shapes=[pltpu.VMEM(features.shape, BF16), pltpu.SemaphoreType.DMA(())],
        compiler_params=pltpu.CompilerParams(vmem_limit_bytes=20 << 20),
        name="feature_copies",
    )(pltpu.with_memory_space_constraint(features, pltpu.HBM))
    source_rows = lax.all_to_all(sent, DST, 0, 0, tiled=True)
    tiles = build(positions, False)
    tile_scratch = [pltpu.VMEM((slots, TILE, TILE), BF16), pltpu.SemaphoreType.DMA((CHUNKS,))]
    partial = spread(
        forward_kernel, "forward_tiles", shape((near, far, TILE, TILE), BF16),
        (index,), tiles, (source_rows,), [pltpu.VMEM((src, TILE, TILE), F32)] + tile_scratch,
    )
    near_parts = lax.all_to_all(partial, NEAR, 0, 0, tiled=True)
    near_sums = jnp.sum(near_parts.astype(F32), axis=0).astype(BF16)
    late_positions, near_sums = lax.optimization_barrier((positions, near_sums))
    back_tiles = build(late_positions, True)
    parts = lax.all_to_all(near_sums, FAR, 0, 0, tiled=True)
    parts, back_tiles = lax.optimization_barrier((parts, back_tiles))
    aggregated = jnp.sum(parts.astype(F32), axis=0).astype(BF16)
    hidden, send, grad_pre = call(
        dense_kernel,
        "dense_layer",
        (shape(grad_out.shape, BF16), shape((far, TILE, TILE), BF16), shape(grad_out.shape, BF16)),
        (),
        (aggregated, weight, bias.reshape(1, -1), grad_out),
    )
    far_rows = lax.all_to_all(send, FAR, 0, 0, tiled=True)
    group = lax.axis_size("d0")
    part = call(part_kernel, "grad_part", shape((2 * TILE + 8, TILE), BF16), (), (aggregated, grad_pre))
    part = lax.all_gather(part, "d0")
    part = call(
        pick_kernel, "grad_pick", shape((2 * TILE // group + 8, TILE), F32), (lax.axis_index("d0").reshape(1),), (part,)
    )
    part = lax.all_gather(part, "x1")
    part = call(
        pick_kernel, "grad_half", shape((TILE // group + 8, TILE), F32), (lax.axis_index("x1").reshape(1),), (part,)
    )
    part = lax.all_gather(part, "x0")
    size = 2 * TILE // dst
    share = call(
        share_kernel, "grad_share", shape((far, size + 8, TILE), BF16), (lax.axis_index("x0").reshape(1),), (part,)
    )
    shared = lax.all_to_all(share, FAR, 0, 0, tiled=True)
    near_all = [far_rows] + [swap(far_rows, k, NEAR) for k in range(1, near)]
    share = call(reshare_kernel, "grad_reshare", shape((near, 2 * size + 8, TILE), BF16), (), (shared,))
    shared = lax.all_to_all(share, NEAR, 0, 0, tiled=True)
    back_send = spread(
        backward_kernel, "backward_tiles", shape((dst, TILE, TILE), BF16),
        (index, lax.axis_index(NEAR).reshape(1)), back_tiles, near_all,
        [pltpu.VMEM((dst, TILE, TILE), F32)] + tile_scratch + [pltpu.VMEM((src, TILE, TILE), BF16)],
    )
    node_scale = 1.0 / math.sqrt(features.shape[0] * src * dst)
    back_send, bias_grad = call(
        lambda *refs: chunk_kernel(*refs, scale=node_scale),
        "grad_chunk",
        (shape((dst, TILE + size, TILE), BF16), shape((1, 2 * TILE), F32)),
        (),
        (shared, back_send),
    )
    received = lax.all_to_all(back_send, DST, 0, 0, tiled=True)
    input_grad, weight_grad = call(
        lambda *refs: final_kernel(*refs, group=group),
        "final_sums",
        (shape(features.shape, BF16), shape((TILE, 2 * TILE), F32)),
        (),
        (received,),
    )
    return (hidden, input_grad, weight_grad, bias_grad.reshape(-1))


def solution(mesh):
    src, dst = mesh.devices.shape
    fine = Mesh(mesh.devices.reshape(2, src // 4, 2, 2, dst // 8, 4), SRC + DST)
    rows = P(SRC + DST, None)
    placed = (
        rows,
        P(),
        P(),
        P(SRC, DST, None),
        P(SRC, DST, None),
        P(SRC, DST, None, None),
        P(SRC, DST, None, None),
        rows,
    )
    return jax.shard_map(
        body, mesh=fine, in_specs=placed, out_specs=(rows, rows, P(), P()), check_vma=False
    )
```

```python
import math

import jax
import jax.numpy as jnp
from jax import lax
from jax.experimental import pallas as pl
from jax.experimental.pallas import tpu as pltpu
from jax.sharding import Mesh, PartitionSpec as P

TILE = 128
BF16 = jnp.bfloat16
F32 = jnp.float32
NN = (((1,), (0,)), ((), ()))
NT = (((1,), (1,)), ((), ()))
TN = (((0,), (0,)), ((), ()))
SRC = ("ylo", "zq", "z0")
DST = ("x1", "x0", "d0")
NEAR = ("ylo", "z0")
FAR = "zq"
GROUP = 32


def dot(a, b, dims=NN):
    return lax.dot_general(a, b, dims, preferred_element_type=F32)


def build_kernel(count_ref, pos_ref, weight_ref, tile_ref, pos_pairs, weight_pairs, *, backward):
    edges, slots = pos_ref.shape
    pairs = slots // 2
    positions = pos_ref[...].T
    weights = weight_ref[...].astype(F32).T
    pos_pairs[...] = jnp.concatenate([positions[:pairs], positions[pairs:]], axis=1)
    weight_pairs[...] = jnp.concatenate([weights[:pairs], weights[pairs:]], axis=1)
    lane = lax.broadcasted_iota(jnp.int32, (1, 2 * edges), 1)
    second = lane >= edges
    half = jnp.where(second, TILE, 0)
    one_rows = lax.broadcasted_iota(jnp.int32, (TILE, 2 * edges), 0)
    two_rows = lax.broadcasted_iota(jnp.int32, (2 * TILE, 2 * edges), 0)

    def one_pair(i, carry):
        limit = jnp.where(second, count_ref[i + pairs] + edges, count_ref[i])
        position = pos_pairs[pl.ds(i, 1), :]
        values = jnp.where(lane < limit, weight_pairs[pl.ds(i, 1), :], 0.0)
        row = position >> 7
        col = position & (TILE - 1)
        if backward:
            left = jnp.where(one_rows == col, 1.0, 0.0).astype(BF16)
            right = jnp.where(two_rows == row + half, values, 0.0).astype(BF16)
        else:
            left = jnp.where(one_rows == row, values, 0.0).astype(BF16)
            right = jnp.where(two_rows == col + half, 1.0, 0.0).astype(BF16)
        both = dot(left, right, NT).astype(BF16)
        tile_ref[i] = both[:, :TILE]
        tile_ref[i + pairs] = both[:, TILE:]
        return carry

    lax.fori_loop(0, pairs, one_pair, 0, unroll=4)


def spread_tiles(index_ref, count_ref, tile_hbm, rows_ref, sums, tile_ref, sems, split, backward, ready):
    shift = split.bit_length() - 1
    starts = range(0, tile_ref.shape[0], GROUP)
    copies = []
    for start in starts:
        part = pl.ds(start, GROUP)
        copies.append(pltpu.make_async_copy(tile_hbm.at[part], tile_ref.at[part], sems.at[start // GROUP]))
    for start in starts:
        pl.when(count_ref[start] > 0)(copies[start // GROUP].start)
    sums[...] = jnp.zeros_like(sums)
    ready()

    def one_group(start):
        copies[start // GROUP].wait()
        found = []
        for slot in range(start, start + GROUP):
            index = index_ref[slot]
            target = index >> shift
            source = index & (split - 1)
            if backward:
                found.append((source, dot(tile_ref[slot], rows_ref[target])))
            else:
                found.append((target, dot(tile_ref[slot], rows_ref[source])))
        for place, value in found:
            sums[place] = sums[place] + value

    for start in starts:
        pl.when(count_ref[start] > 0)(lambda start=start: one_group(start))


def forward_kernel(index_ref, count_ref, tile_hbm, rows_ref, out_ref, sums, tile_ref, sems):
    near, far = out_ref.shape[:2]
    split = rows_ref.shape[0]
    spread_tiles(index_ref, count_ref, tile_hbm, rows_ref, sums, tile_ref, sems, split, False, lambda: None)
    for target in range(near * far):
        place = target // (2 * far) * 2 + target % 2
        out_ref[place, target // 2 % far] = sums[target].astype(BF16)


def high_low(value):
    high = value.astype(BF16).astype(F32)
    return high, value - high


def bias_tile(bias_rows):
    high, low = high_low(bias_rows[0:2])
    return jnp.concatenate([high, low, jnp.zeros((4, TILE), F32)], axis=0).astype(BF16)


def bias_sum(tile):
    return tile[0:2] + tile[2:4]


def dense_kernel(agg_ref, weight_ref, bias_ref, grad_ref, hidden_ref, send_ref, grad_pre_ref):
    aggregated = agg_ref[...]
    weight = weight_ref[...]
    preact = dot(aggregated, weight) + bias_ref[...]
    sigma = 1.0 / (1.0 + jnp.exp(-preact))
    hidden_ref[...] = (preact * sigma).astype(BF16)
    grad_pre = (grad_ref[...].astype(F32) * sigma * (1.0 + preact * (1.0 - sigma))).astype(BF16)
    grad_pre_ref[...] = grad_pre
    back_rows = dot(grad_pre, weight, NT).astype(BF16)
    send_ref[...] = jnp.broadcast_to(back_rows[None], send_ref.shape)


def part_kernel(agg_ref, grad_pre_ref, out_ref):
    grad_pre = grad_pre_ref[...]
    part = dot(agg_ref[...], grad_pre, TN).astype(BF16)
    out_ref[:TILE] = part[:, :TILE]
    out_ref[TILE : 2 * TILE] = part[:, TILE:]
    bias_part = jnp.sum(grad_pre.astype(F32), axis=0, keepdims=True)
    out_ref[2 * TILE :] = bias_tile(jnp.concatenate([bias_part[:, :TILE], bias_part[:, TILE:]], axis=0))


def pick_rows(place, recv_ref, size):
    peers = recv_ref.shape[0]
    start = pl.multiple_of(place * size, 8)
    total = recv_ref[0, pl.ds(start, size), :].astype(F32)
    last = recv_ref[0, peers * size :, :].astype(F32)
    for k in range(1, peers):
        total = total + recv_ref[k, pl.ds(start, size), :].astype(F32)
        last = last + recv_ref[k, peers * size :, :].astype(F32)
    return total, last


def pick_kernel(place_ref, recv_ref, out_ref):
    size = out_ref.shape[0] - 8
    out_ref[:size], out_ref[size:] = pick_rows(place_ref[0], recv_ref, size)


def share_kernel(place_ref, part_ref, out_ref):
    size = (part_ref.shape[1] - 8) // part_ref.shape[0]
    total, last = pick_rows(place_ref[0], part_ref, size)
    rows = jnp.concatenate([total.astype(BF16), bias_tile(bias_sum(last))], axis=0)
    out_ref[...] = jnp.broadcast_to(rows[None], out_ref.shape)


def reshare_kernel(recv_ref, out_ref):
    total = jnp.sum(recv_ref[...].astype(F32), axis=0)
    size = (out_ref.shape[1] - 8) // 2
    high, low = high_low(total[:size])
    rows = [high.astype(BF16), low.astype(BF16), bias_tile(bias_sum(total[size:]))]
    out_ref[...] = jnp.broadcast_to(jnp.concatenate(rows, axis=0)[None], out_ref.shape)


def chunk_kernel(recv_ref, back_ref, out_ref, bias_grad_ref, *, scale):
    total = jnp.sum(recv_ref[...].astype(F32), axis=0) * scale
    size = (total.shape[0] - 8) // 2
    bias_rows = bias_sum(total[2 * size :])
    bias_grad_ref[:, :TILE] = bias_rows[0:1]
    bias_grad_ref[:, TILE:] = bias_rows[1:2]
    chunk = (total[:size] + total[size : 2 * size]).astype(BF16)
    out_ref[:, :TILE, :] = back_ref[...]
    out_ref[:, TILE:, :] = jnp.broadcast_to(chunk[None], (out_ref.shape[0], size, TILE))


def copies_kernel(rows_hbm, out_ref, rows_ref, sem):
    copy = pltpu.make_async_copy(rows_hbm, rows_ref, sem)
    copy.start()
    copy.wait()
    out_ref[...] = jnp.broadcast_to(rows_ref[...][None], out_ref.shape)


def final_kernel(recv_ref, input_ref, weight_grad_ref, *, group):
    pieces = recv_ref.shape[0]
    input_ref[...] = jnp.sum(recv_ref[:, :TILE, :].astype(F32), axis=0).astype(BF16)
    size = 2 * TILE // pieces
    for d in range(pieces):
        start = ((d % group) * (pieces // group) + d // group) * size
        chunk = recv_ref[d, TILE:, :].astype(F32)
        lane = start // TILE * TILE
        weight_grad_ref[start % TILE : start % TILE + size, lane : lane + TILE] = chunk


def backward_kernel(index_ref, count_ref, own_ref, tile_hbm, *rest):
    near_refs, (out_ref, sums, tile_ref, sems, rows) = rest[:-5], rest[-5:]
    far = near_refs[0].shape[0]
    pieces = out_ref.shape[0]

    def ready():
        for k, near_ref in enumerate(near_refs):
            other = own_ref[0] ^ k
            base = (other >> 1) * (2 * far) + (other & 1)
            for q in range(far):
                rows[base + 2 * q] = near_ref[q]

    spread_tiles(index_ref, count_ref, tile_hbm, rows, sums, tile_ref, sems, pieces, True, ready)
    out_ref[...] = sums[...].astype(BF16)


def vmem(n):
    return [pl.BlockSpec(memory_space=pltpu.VMEM)] * n


def smem(n):
    return [pl.BlockSpec(memory_space=pltpu.SMEM)] * n


def call(kernel, name, outs, scalars, arrays, scratch=(), **more):
    single = not isinstance(outs, tuple)
    return pl.pallas_call(
        kernel,
        out_shape=outs,
        in_specs=smem(len(scalars)) + vmem(len(arrays)),
        out_specs=vmem(1)[0] if single else tuple(vmem(len(outs))),
        scratch_shapes=list(scratch),
        compiler_params=pltpu.CompilerParams(vmem_limit_bytes=20 << 20),
        name=name,
        **more,
    )(*scalars, *arrays)


def shape(dims, dtype):
    return jax.ShapeDtypeStruct(dims, dtype)


def spread(kernel, name, out, scalars, tiles, arrays, scratch):
    return pl.pallas_call(
        kernel,
        out_shape=out,
        in_specs=smem(len(scalars)) + [pl.BlockSpec(memory_space=pltpu.HBM)] + vmem(len(arrays)),
        out_specs=vmem(1)[0],
        scratch_shapes=scratch,
        compiler_params=pltpu.CompilerParams(vmem_limit_bytes=20 << 20),
        name=name,
    )(*scalars, pltpu.with_memory_space_constraint(tiles, pltpu.HBM), *arrays)


def swap(array, step, axis):
    return lax.ppermute(array, axis, [(i, i ^ step) for i in range(lax.axis_size(axis))])


def body(features, weight, bias, tile_index, edge_count, edge_pos, edge_weight, grad_out):
    near = lax.axis_size(NEAR)
    far = lax.axis_size(FAR)
    src = near * far
    dst = lax.axis_size(DST)
    index = tile_index.reshape(-1)
    counts = edge_count.reshape(-1)
    slots = counts.shape[0]
    positions = edge_pos.reshape(slots, -1).T
    weights = edge_weight.reshape(slots, -1).T
    edges = positions.shape[0]
    tile_shape = pltpu.HBM((slots, TILE, TILE), BF16)
    pair_scratch = (pltpu.VMEM((slots // 2, 2 * edges), jnp.int32), pltpu.VMEM((slots // 2, 2 * edges), F32))

    def build(positions, backward):
        return call(
            lambda *refs: build_kernel(*refs, backward=backward),
            "build_back" if backward else "build_tiles",
            tile_shape, (counts,), (positions, weights), pair_scratch,
        )

    sent = pl.pallas_call(
        copies_kernel,
        out_shape=shape((dst,) + features.shape, BF16),
        in_specs=[pl.BlockSpec(memory_space=pltpu.HBM)],
        out_specs=vmem(1)[0],
        scratch_shapes=[pltpu.VMEM(features.shape, BF16), pltpu.SemaphoreType.DMA(())],
        compiler_params=pltpu.CompilerParams(vmem_limit_bytes=20 << 20),
        name="feature_copies",
    )(pltpu.with_memory_space_constraint(features, pltpu.HBM))
    source_rows = lax.all_to_all(sent, DST, 0, 0, tiled=True)
    tiles = build(positions, False)
    tile_scratch = [pltpu.VMEM((slots, TILE, TILE), BF16), pltpu.SemaphoreType.DMA((slots // GROUP,))]
    partial = spread(
        forward_kernel, "forward_tiles", shape((near, far, TILE, TILE), BF16),
        (index, counts), tiles, (source_rows,), [pltpu.VMEM((src, TILE, TILE), F32)] + tile_scratch,
    )
    near_parts = lax.all_to_all(partial, NEAR, 0, 0, tiled=True)
    near_sums = jnp.sum(near_parts.astype(F32), axis=0).astype(BF16)
    late_positions, near_sums = lax.optimization_barrier((positions, near_sums))
    back_tiles = build(late_positions, True)
    parts = lax.all_to_all(near_sums, FAR, 0, 0, tiled=True)
    parts, back_tiles = lax.optimization_barrier((parts, back_tiles))
    aggregated = jnp.sum(parts.astype(F32), axis=0).astype(BF16)
    hidden, send, grad_pre = call(
        dense_kernel,
        "dense_layer",
        (shape(grad_out.shape, BF16), shape((far, TILE, TILE), BF16), shape(grad_out.shape, BF16)),
        (),
        (aggregated, weight, bias.reshape(1, -1), grad_out),
    )
    far_rows = lax.all_to_all(send, FAR, 0, 0, tiled=True)
    group = lax.axis_size("d0")
    part = call(part_kernel, "grad_part", shape((2 * TILE + 8, TILE), BF16), (), (aggregated, grad_pre))
    part = lax.all_gather(part, "d0")
    part = call(
        pick_kernel, "grad_pick", shape((2 * TILE // group + 8, TILE), F32), (lax.axis_index("d0").reshape(1),), (part,)
    )
    part = lax.all_gather(part, "x1")
    part = call(
        pick_kernel, "grad_half", shape((TILE // group + 8, TILE), F32), (lax.axis_index("x1").reshape(1),), (part,)
    )
    part = lax.all_gather(part, "x0")
    size = 2 * TILE // dst
    share = call(
        share_kernel, "grad_share", shape((far, size + 8, TILE), BF16), (lax.axis_index("x0").reshape(1),), (part,)
    )
    shared = lax.all_to_all(share, FAR, 0, 0, tiled=True)
    near_all = [far_rows] + [swap(far_rows, k, NEAR) for k in range(1, near)]
    share = call(reshare_kernel, "grad_reshare", shape((near, 2 * size + 8, TILE), BF16), (), (shared,))
    shared = lax.all_to_all(share, NEAR, 0, 0, tiled=True)
    back_send = spread(
        backward_kernel, "backward_tiles", shape((dst, TILE, TILE), BF16),
        (index, counts, lax.axis_index(NEAR).reshape(1)), back_tiles, near_all,
        [pltpu.VMEM((dst, TILE, TILE), F32)] + tile_scratch + [pltpu.VMEM((src, TILE, TILE), BF16)],
    )
    node_scale = 1.0 / math.sqrt(features.shape[0] * src * dst)
    back_send, bias_grad = call(
        lambda *refs: chunk_kernel(*refs, scale=node_scale),
        "grad_chunk",
        (shape((dst, TILE + size, TILE), BF16), shape((1, 2 * TILE), F32)),
        (),
        (shared, back_send),
    )
    received = lax.all_to_all(back_send, DST, 0, 0, tiled=True)
    input_grad, weight_grad = call(
        lambda *refs: final_kernel(*refs, group=group),
        "final_sums",
        (shape(features.shape, BF16), shape((TILE, 2 * TILE), F32)),
        (),
        (received,),
    )
    return (hidden, input_grad, weight_grad, bias_grad.reshape(-1))


def solution(mesh):
    src, dst = mesh.devices.shape
    fine = Mesh(mesh.devices.reshape(2, src // 4, 2, 2, dst // 8, 4), SRC + DST)
    rows = P(SRC + DST, None)
    placed = (
        rows,
        P(),
        P(),
        P(SRC, DST, None),
        P(SRC, DST, None),
        P(SRC, DST, None, None),
        P(SRC, DST, None, None),
        rows,
    )
    return jax.shard_map(
        body, mesh=fine, in_specs=placed, out_specs=(rows, rows, P(), P()), check_vma=False
    )
```

```python
import math

import jax
import jax.numpy as jnp
from jax import lax
from jax.experimental import pallas as pl
from jax.experimental.pallas import tpu as pltpu
from jax.sharding import Mesh, PartitionSpec as P

TILE = 128
BF16 = jnp.bfloat16
F32 = jnp.float32
NN = (((1,), (0,)), ((), ()))
NT = (((1,), (1,)), ((), ()))
TN = (((0,), (0,)), ((), ()))
SRC = ("ylo", "zq", "z0")
DST = ("x1", "x0", "d0")
NEAR = ("ylo", "z0")
FAR = "zq"
GROUP = 32


def dot(a, b, dims=NN):
    return lax.dot_general(a, b, dims, preferred_element_type=F32)


def build_kernel(count_ref, pos_ref, weight_ref, tile_ref, pos_pairs, weight_pairs, *, backward):
    edges, slots = pos_ref.shape
    pairs = slots // 2
    positions = pos_ref[...].T
    weights = weight_ref[...].astype(F32).T
    pos_pairs[...] = jnp.concatenate([positions[:pairs], positions[pairs:]], axis=1)
    weight_pairs[...] = jnp.concatenate([weights[:pairs], weights[pairs:]], axis=1)
    lane = lax.broadcasted_iota(jnp.int32, (1, 2 * edges), 1)
    second = lane >= edges
    half = jnp.where(second, TILE, 0)
    one_rows = lax.broadcasted_iota(jnp.int32, (TILE, 2 * edges), 0)
    two_rows = lax.broadcasted_iota(jnp.int32, (2 * TILE, 2 * edges), 0)

    def one_pair(i, carry):
        limit = jnp.where(second, count_ref[i + pairs] + edges, count_ref[i])
        position = pos_pairs[pl.ds(i, 1), :]
        values = jnp.where(lane < limit, weight_pairs[pl.ds(i, 1), :], 0.0)
        row = position >> 7
        col = position & (TILE - 1)
        if backward:
            left = jnp.where(one_rows == col, 1.0, 0.0).astype(BF16)
            right = jnp.where(two_rows == row + half, values, 0.0).astype(BF16)
        else:
            left = jnp.where(one_rows == row, values, 0.0).astype(BF16)
            right = jnp.where(two_rows == col + half, 1.0, 0.0).astype(BF16)
        both = dot(left, right, NT).astype(BF16)
        tile_ref[i] = both[:, :TILE]
        tile_ref[i + pairs] = both[:, TILE:]
        return carry

    lax.fori_loop(0, pairs, one_pair, 0, unroll=4)


def spread_tiles(index_ref, count_ref, tile_hbm, rows_ref, sums, tile_ref, sems, split, backward, ready):
    shift = split.bit_length() - 1
    starts = range(0, tile_ref.shape[0], GROUP)
    copies = []
    for start in starts:
        part = pl.ds(start, GROUP)
        copies.append(pltpu.make_async_copy(tile_hbm.at[part], tile_ref.at[part], sems.at[start // GROUP]))
    for start in starts:
        pl.when(count_ref[start] > 0)(copies[start // GROUP].start)
    sums[...] = jnp.zeros_like(sums)
    ready()

    def one_group(start):
        copies[start // GROUP].wait()
        found = []
        for slot in range(start, start + GROUP):
            index = index_ref[slot]
            target = index >> shift
            source = index & (split - 1)
            if backward:
                found.append((source, dot(tile_ref[slot], rows_ref[target])))
            else:
                found.append((target, dot(tile_ref[slot], rows_ref[source])))
        for place, value in found:
            sums[place] = sums[place] + value

    for start in starts:
        pl.when(count_ref[start] > 0)(lambda start=start: one_group(start))


def forward_kernel(index_ref, count_ref, tile_hbm, rows_ref, out_ref, sums, tile_ref, sems):
    near, far = out_ref.shape[:2]
    split = rows_ref.shape[0]
    spread_tiles(index_ref, count_ref, tile_hbm, rows_ref, sums, tile_ref, sems, split, False, lambda: None)
    for target in range(near * far):
        place = target // (2 * far) * 2 + target % 2
        out_ref[place, target // 2 % far] = sums[target].astype(BF16)


def high_low(value):
    high = value.astype(BF16).astype(F32)
    return high, value - high


def bias_tile(bias_rows):
    high, low = high_low(bias_rows[0:2])
    return jnp.concatenate([high, low, jnp.zeros((4, TILE), F32)], axis=0).astype(BF16)


def bias_sum(tile):
    return tile[0:2] + tile[2:4]


def dense_kernel(agg_ref, weight_ref, bias_ref, grad_ref, hidden_ref, send_ref, grad_pre_ref):
    aggregated = agg_ref[...]
    weight = weight_ref[...]
    preact = dot(aggregated, weight) + bias_ref[...]
    sigma = 1.0 / (1.0 + jnp.exp(-preact))
    hidden_ref[...] = (preact * sigma).astype(BF16)
    grad_pre = (grad_ref[...].astype(F32) * sigma * (1.0 + preact * (1.0 - sigma))).astype(BF16)
    grad_pre_ref[...] = grad_pre
    back_rows = dot(grad_pre, weight, NT).astype(BF16)
    send_ref[...] = jnp.broadcast_to(back_rows[None], send_ref.shape)


def part_kernel(agg_ref, grad_pre_ref, out_ref):
    grad_pre = grad_pre_ref[...]
    part = dot(agg_ref[...], grad_pre, TN).astype(BF16)
    out_ref[:TILE] = part[:, :TILE]
    out_ref[TILE : 2 * TILE] = part[:, TILE:]
    bias_part = jnp.sum(grad_pre.astype(F32), axis=0, keepdims=True)
    out_ref[2 * TILE :] = bias_tile(jnp.concatenate([bias_part[:, :TILE], bias_part[:, TILE:]], axis=0))


def pick_rows(place, recv_ref, size):
    peers = recv_ref.shape[0]
    start = pl.multiple_of(place * size, 8)
    total = recv_ref[0, pl.ds(start, size), :].astype(F32)
    last = recv_ref[0, peers * size :, :].astype(F32)
    for k in range(1, peers):
        total = total + recv_ref[k, pl.ds(start, size), :].astype(F32)
        last = last + recv_ref[k, peers * size :, :].astype(F32)
    return total, last


def pick_kernel(place_ref, recv_ref, out_ref):
    size = out_ref.shape[0] - 8
    out_ref[:size], out_ref[size:] = pick_rows(place_ref[0], recv_ref, size)


def share_kernel(place_ref, part_ref, out_ref):
    size = (part_ref.shape[1] - 8) // part_ref.shape[0]
    total, last = pick_rows(place_ref[0], part_ref, size)
    rows = jnp.concatenate([total.astype(BF16), bias_tile(bias_sum(last))], axis=0)
    out_ref[...] = jnp.broadcast_to(rows[None], out_ref.shape)


def reshare_kernel(recv_ref, out_ref):
    total = jnp.sum(recv_ref[...].astype(F32), axis=0)
    size = (out_ref.shape[1] - 8) // 2
    high, low = high_low(total[:size])
    rows = [high.astype(BF16), low.astype(BF16), bias_tile(bias_sum(total[size:]))]
    out_ref[...] = jnp.broadcast_to(jnp.concatenate(rows, axis=0)[None], out_ref.shape)


def chunk_kernel(recv_ref, back_ref, out_ref, bias_grad_ref, *, scale):
    total = jnp.sum(recv_ref[...].astype(F32), axis=0) * scale
    size = (total.shape[0] - 8) // 2
    bias_rows = bias_sum(total[2 * size :])
    bias_grad_ref[:, :TILE] = bias_rows[0:1]
    bias_grad_ref[:, TILE:] = bias_rows[1:2]
    chunk = (total[:size] + total[size : 2 * size]).astype(BF16)
    out_ref[:, :TILE, :] = back_ref[...]
    out_ref[:, TILE:, :] = jnp.broadcast_to(chunk[None], (out_ref.shape[0], size, TILE))


def copies_kernel(rows_ref, out_ref):
    out_ref[...] = jnp.broadcast_to(rows_ref[...][None], out_ref.shape)


def final_kernel(recv_ref, input_ref, weight_grad_ref, *, group):
    pieces = recv_ref.shape[0]
    input_ref[...] = jnp.sum(recv_ref[:, :TILE, :].astype(F32), axis=0).astype(BF16)
    size = 2 * TILE // pieces
    for d in range(pieces):
        start = ((d % group) * (pieces // group) + d // group) * size
        chunk = recv_ref[d, TILE:, :].astype(F32)
        lane = start // TILE * TILE
        weight_grad_ref[start % TILE : start % TILE + size, lane : lane + TILE] = chunk


def backward_kernel(index_ref, count_ref, own_ref, tile_hbm, *rest):
    near_refs, (out_ref, sums, tile_ref, sems, rows) = rest[:-5], rest[-5:]
    far = near_refs[0].shape[0]
    pieces = out_ref.shape[0]

    def ready():
        for k, near_ref in enumerate(near_refs):
            other = own_ref[0] ^ k
            base = (other >> 1) * (2 * far) + (other & 1)
            for q in range(far):
                rows[base + 2 * q] = near_ref[q]

    spread_tiles(index_ref, count_ref, tile_hbm, rows, sums, tile_ref, sems, pieces, True, ready)
    out_ref[...] = sums[...].astype(BF16)


def vmem(n):
    return [pl.BlockSpec(memory_space=pltpu.VMEM)] * n


def smem(n):
    return [pl.BlockSpec(memory_space=pltpu.SMEM)] * n


def call(kernel, name, outs, scalars, arrays, scratch=(), **more):
    single = not isinstance(outs, tuple)
    return pl.pallas_call(
        kernel,
        out_shape=outs,
        in_specs=smem(len(scalars)) + vmem(len(arrays)),
        out_specs=vmem(1)[0] if single else tuple(vmem(len(outs))),
        scratch_shapes=list(scratch),
        compiler_params=pltpu.CompilerParams(vmem_limit_bytes=20 << 20),
        name=name,
        **more,
    )(*scalars, *arrays)


def shape(dims, dtype):
    return jax.ShapeDtypeStruct(dims, dtype)


def spread(kernel, name, out, scalars, tiles, arrays, scratch):
    return pl.pallas_call(
        kernel,
        out_shape=out,
        in_specs=smem(len(scalars)) + [pl.BlockSpec(memory_space=pltpu.HBM)] + vmem(len(arrays)),
        out_specs=vmem(1)[0],
        scratch_shapes=scratch,
        compiler_params=pltpu.CompilerParams(vmem_limit_bytes=20 << 20),
        name=name,
    )(*scalars, pltpu.with_memory_space_constraint(tiles, pltpu.HBM), *arrays)


def swap(array, step, axis):
    return lax.ppermute(array, axis, [(i, i ^ step) for i in range(lax.axis_size(axis))])


def body(features, weight, bias, tile_index, edge_count, edge_pos, edge_weight, grad_out):
    near = lax.axis_size(NEAR)
    far = lax.axis_size(FAR)
    src = near * far
    dst = lax.axis_size(DST)
    index = tile_index.reshape(-1)
    counts = edge_count.reshape(-1)
    slots = counts.shape[0]
    positions = edge_pos.reshape(slots, -1).T
    weights = edge_weight.reshape(slots, -1).T
    edges = positions.shape[0]
    tile_shape = pltpu.HBM((slots, TILE, TILE), BF16)
    pair_scratch = (pltpu.VMEM((slots // 2, 2 * edges), jnp.int32), pltpu.VMEM((slots // 2, 2 * edges), F32))

    def build(positions, backward):
        return call(
            lambda *refs: build_kernel(*refs, backward=backward),
            "build_back" if backward else "build_tiles",
            tile_shape, (counts,), (positions, weights), pair_scratch,
        )

    sent = call(copies_kernel, "feature_copies", shape((dst,) + features.shape, BF16), (), (features,))
    source_rows = lax.all_to_all(sent, DST, 0, 0, tiled=True)
    tiles = build(positions, False)
    tile_scratch = [pltpu.VMEM((slots, TILE, TILE), BF16), pltpu.SemaphoreType.DMA((slots // GROUP,))]
    partial = spread(
        forward_kernel, "forward_tiles", shape((near, far, TILE, TILE), BF16),
        (index, counts), tiles, (source_rows,), [pltpu.VMEM((src, TILE, TILE), F32)] + tile_scratch,
    )
    near_parts = lax.all_to_all(partial, NEAR, 0, 0, tiled=True)
    near_sums = jnp.sum(near_parts.astype(F32), axis=0).astype(BF16)
    late_positions, near_sums = lax.optimization_barrier((positions, near_sums))
    back_tiles = build(late_positions, True)
    parts = lax.all_to_all(near_sums, FAR, 0, 0, tiled=True)
    parts, back_tiles = lax.optimization_barrier((parts, back_tiles))
    aggregated = jnp.sum(parts.astype(F32), axis=0).astype(BF16)
    hidden, send, grad_pre = call(
        dense_kernel,
        "dense_layer",
        (shape(grad_out.shape, BF16), shape((far, TILE, TILE), BF16), shape(grad_out.shape, BF16)),
        (),
        (aggregated, weight, bias.reshape(1, -1), grad_out),
    )
    far_rows = lax.all_to_all(send, FAR, 0, 0, tiled=True)
    group = lax.axis_size("d0")
    part = call(part_kernel, "grad_part", shape((2 * TILE + 8, TILE), BF16), (), (aggregated, grad_pre))
    part = lax.all_gather(part, "d0")
    part = call(
        pick_kernel, "grad_pick", shape((2 * TILE // group + 8, TILE), F32), (lax.axis_index("d0").reshape(1),), (part,)
    )
    part = lax.all_gather(part, "x1")
    part = call(
        pick_kernel, "grad_half", shape((TILE // group + 8, TILE), F32), (lax.axis_index("x1").reshape(1),), (part,)
    )
    part = lax.all_gather(part, "x0")
    size = 2 * TILE // dst
    share = call(
        share_kernel, "grad_share", shape((far, size + 8, TILE), BF16), (lax.axis_index("x0").reshape(1),), (part,)
    )
    shared = lax.all_to_all(share, FAR, 0, 0, tiled=True)
    near_all = [far_rows] + [swap(far_rows, k, NEAR) for k in range(1, near)]
    share = call(reshare_kernel, "grad_reshare", shape((near, 2 * size + 8, TILE), BF16), (), (shared,))
    shared = lax.all_to_all(share, NEAR, 0, 0, tiled=True)
    back_send = spread(
        backward_kernel, "backward_tiles", shape((dst, TILE, TILE), BF16),
        (index, counts, lax.axis_index(NEAR).reshape(1)), back_tiles, near_all,
        [pltpu.VMEM((dst, TILE, TILE), F32)] + tile_scratch + [pltpu.VMEM((src, TILE, TILE), BF16)],
    )
    node_scale = 1.0 / math.sqrt(features.shape[0] * src * dst)
    back_send, bias_grad = call(
        lambda *refs: chunk_kernel(*refs, scale=node_scale),
        "grad_chunk",
        (shape((dst, TILE + size, TILE), BF16), shape((1, 2 * TILE), F32)),
        (),
        (shared, back_send),
    )
    received = lax.all_to_all(back_send, DST, 0, 0, tiled=True)
    input_grad, weight_grad = call(
        lambda *refs: final_kernel(*refs, group=group),
        "final_sums",
        (shape(features.shape, BF16), shape((TILE, 2 * TILE), F32)),
        (),
        (received,),
    )
    return (hidden, input_grad, weight_grad, bias_grad.reshape(-1))


def solution(mesh):
    src, dst = mesh.devices.shape
    fine = Mesh(mesh.devices.reshape(2, src // 4, 2, 2, dst // 8, 4), SRC + DST)
    rows = P(SRC + DST, None)
    placed = (
        rows,
        P(),
        P(),
        P(SRC, DST, None),
        P(SRC, DST, None),
        P(SRC, DST, None, None),
        P(SRC, DST, None, None),
        rows,
    )
    return jax.shard_map(
        body, mesh=fine, in_specs=placed, out_specs=(rows, rows, P(), P()), check_vma=False
    )
```
